128 devices in a mesh: mod: 8 (over z, core), row: 16 (over x, y).
Axes of the slice: x: 4, y: 4, z: 4, core: 2. Of those that a mesh axis runs over, the one named last changes fastest.
Arguments:
- activations: bfloat16 [8, 16384, 4096], P('mod', 'row'), may hold values from -6 to 6
- out_grads: bfloat16 [8, 16384, 4096], P('mod', 'row'), may hold values from -0.3125 to 0.3125
- in_projection: bfloat16 [8, 64, 4096], P('mod'), may hold values from -0.09375 to 0.09375
- out_projection: bfloat16 [8, 64, 4096], P('mod'), may hold values from -0.09375 to 0.09375
- inv_curvature: bfloat16 [8, 4096, 4096], P('mod', 'row'), as said below
- store_grads: bfloat16 [8, 12288, 4096], P('mod', 'row'), may hold values from -0.03125 to 0.03125
- lengths: int32 [64], replicated, may hold values from 64 to 128, as said below
- owners: int32 [64], replicated, may hold values from 0 to 15, as said below
Outputs:
- scores: float32 [64, 12288], P('mod', 'row')
The draws below stay inside these ranges and needn't reach their ends.
Inputs may be any that keep to these rules, and one draw needn't show every extreme that they name: `owners`: at most 8 query examples have the same owner, and some owner has exactly 8. `lengths`: the examples of one owner hold at most 1024 tokens together, and some owner holds exactly 1024. `inv_curvature`: each module's matrix is symmetric.
All inputs are finite; a program needn't handle non-finite values.
Results may differ from the reference program's by a relative error of at most 0.0041.
Values may be sent and summed in bfloat16 or wider, within the bound.
A program may use at most 128 MiB of HBM per device.

```python
import math
import jax
import jax.numpy as jnp
import numpy as np
from jax import lax

D = 4096
RANK = 64
LEN = 128
MODS = 8
QUERIES = 64
TOK_DEV = 1024
TOKENS = 16384
STORE = 12288
K = 4096
N_ROW = 16


def routing_plan(key):
    base = jax.random.fold_in(key, 23)
    key_owner, key_example, key_length = jax.random.split(base, 3)
    mean = QUERIES // N_ROW
    pattern = np.array([2 * mean, mean, mean // 2, mean // 2])
    per_slot = np.tile(pattern, N_ROW // 4)
    slot_of_rank = np.repeat(np.arange(N_ROW), per_slot)
    shuffled_owners = jax.random.permutation(key_owner, N_ROW).astype(jnp.int32)
    shuffled_examples = jax.random.permutation(key_example, QUERIES)
    owner_by_rank = shuffled_owners[jnp.asarray(slot_of_rank, dtype=jnp.int32)]
    owners = jnp.zeros((QUERIES,), jnp.int32).at[shuffled_examples].set(owner_by_rank)
    drawn = jax.random.randint(key_length, (QUERIES,), LEN // 2, LEN + 1).astype(jnp.int32)
    length_by_rank = jnp.where(jnp.asarray(slot_of_rank == 0), LEN, drawn).astype(jnp.int32)
    lengths = jnp.zeros((QUERIES,), jnp.int32).at[shuffled_examples].set(length_by_rank)
    return (owners, lengths)


def draw_owners(key, part):
    return routing_plan(key)[0]


def draw_lengths(key, part):
    return routing_plan(key)[1]


def draw_inv_curvature(key, part):
    key_noise, key_diag = jax.random.split(jax.random.fold_in(key, 11), 2)
    order = RANK * RANK
    noise = jax.random.normal(key_noise, (MODS, order, order), jnp.float32)
    noise = (noise + jnp.swapaxes(noise, 1, 2)) * (0.4 / math.sqrt(2.0 * order))
    diagonal = jnp.exp(jax.random.uniform(key_diag, (MODS, order), jnp.float32, 0.0, math.log(3.0)))
    index = jnp.arange(order, dtype=jnp.int32)
    on_diag = (index[:, None] == index[None, :]).astype(jnp.float32)
    matrix = noise + diagonal[:, :, None] * on_diag[None, :, :]
    return matrix.astype(jnp.bfloat16)


def levels(rng, dims, cuts, smallest, high):
    level = 1.0
    for axis_at, blocks in cuts:
        draws = jax.random.uniform(jax.random.fold_in(jax.random.fold_in(rng, 6), axis_at), (blocks,), jnp.float32, smallest / len(cuts), high / len(cuts))
        level = level * jnp.repeat(jnp.exp(draws), dims[axis_at] // blocks).reshape((-1,) + (1,) * (len(dims) - 1 - axis_at))
    return level


def normal_values(stream_key, extent, deviation, bound, pieces=(), kind=jnp.bfloat16):
    values = deviation * jax.random.normal(stream_key, extent, jnp.float32)
    if pieces:
        values = values * levels(stream_key, extent, pieces, -0.22, 0.18)
    return jnp.clip(values, -bound, bound).astype(kind)


def setup_inputs(seed: int = 0) -> dict:
    splits = jax.random.split(jax.random.key(seed), 9)
    activations = normal_values(splits[0], (MODS, TOKENS, D), 1.0, 6.0, ((0, 8), (1, 16)))
    out_grads = normal_values(splits[1], (MODS, TOKENS, D), 0.05, 0.3125, ((0, 8), (1, 16)))
    in_projection = normal_values(splits[2], (MODS, RANK, D), D ** -0.5, 0.09375, ((0, 8),))
    out_projection = normal_values(splits[3], (MODS, RANK, D), D ** -0.5, 0.09375, ((0, 8),))
    inv_curvature = draw_inv_curvature(jax.random.fold_in(splits[8], 71), 0)
    store_grads = normal_values(splits[5], (MODS, STORE, K), (K * MODS) ** -0.5, 0.03125, ((0, 8), (1, 16)))
    lengths = draw_lengths(jax.random.fold_in(splits[8], 71), 0)
    owners = draw_owners(jax.random.fold_in(splits[8], 71), 0)
    return dict(activations=activations, out_grads=out_grads, in_projection=in_projection, out_projection=out_projection, inv_curvature=inv_curvature, store_grads=store_grads, lengths=lengths, owners=owners)


exact_mode = lax.Precision.HIGHEST


def contract_last(left, right):
    return lax.dot_general(left, right, (((1,), (1,)), ((), ())), preferred_element_type=jnp.float32)


def reference(activations, out_grads, in_projection, out_projection, inv_curvature, store_grads, lengths, owners):
    examples = jnp.arange(QUERIES, dtype=jnp.int32)
    earlier = (owners[:, None] == owners[None, :]) & (examples[None, :] < examples[:, None])
    offsets = jnp.sum(jnp.where(earlier, lengths[None, :], 0), axis=1).astype(jnp.int32)
    positions = jnp.arange(TOKENS, dtype=jnp.int32)
    row_owner = positions // TOK_DEV
    row_local = positions % TOK_DEV
    membership = ((owners[:, None] == row_owner[None, :])
                  & (row_local[None, :] >= offsets[:, None])
                  & (row_local[None, :] < (offsets + lengths)[:, None])).astype(jnp.float32)

    def one_module(module):
        in_feat = contract_last(activations[module], in_projection[module])
        out_feat = contract_last(out_grads[module], out_projection[module])
        weighted = membership[:, None, :] * out_feat.T[None, :, :]
        per_example = jnp.dot(weighted.reshape(QUERIES * RANK, TOKENS), in_feat, precision=exact_mode)
        feature = per_example.reshape(QUERIES, K).astype(jnp.bfloat16)
        preconditioned = jnp.dot(feature, inv_curvature[module], preferred_element_type=jnp.float32).astype(jnp.bfloat16)
        return contract_last(preconditioned, store_grads[module])

    module_scores = lax.map(one_module, jnp.arange(MODS, dtype=jnp.int32))
    return jnp.sum(module_scores, axis=0)
```

```python
import functools

import jax
import jax.numpy as jnp
from jax import lax
from jax.experimental import pallas as pl
from jax.experimental.pallas import tpu as pltpu
from jax.sharding import PartitionSpec as P

f32, bf16 = jnp.float32, jnp.bfloat16
CAP = 8
LEN_MAX, LEN_MIN = 128, 64
TILES = 4
SIDE = 4


def dot_nt(a, b):
    return lax.dot_general(a, b, (((1,), (1,)), ((), ())), preferred_element_type=f32)


def dot_nn(a, b):
    return lax.dot_general(a, b, (((1,), (0,)), ((), ())), preferred_element_type=f32)


def halves(x):
    hi = x.astype(bf16)
    return hi, (x - hi.astype(f32)).astype(bf16)


def remote(src, dst, send, recv, axis, peer):
    return pltpu.make_async_remote_copy(
        src_ref=src, dst_ref=dst, send_sem=send, recv_sem=recv,
        device_id={axis: peer}, device_id_type=pl.DeviceIdType.MESH,
    )


def row_of(x, y):
    return x * SIDE + y


class Gather:
    def __init__(self, part, send, recv, x, y):
        self.part, self.send, self.recv, self.x, self.y = part, send, recv, x, y
        self.started = []

    def coord(self, h, d):
        x, y = self.x, self.y
        if h == 0:
            return row_of(x, lax.rem(y + d, SIDE))
        return row_of(lax.rem(x + d, SIDE), y)

    def src(self, h, d1, d2):
        if h == 0:
            return row_of(lax.rem(self.x + d2, SIDE), lax.rem(self.y + d1, SIDE))
        return row_of(lax.rem(self.x + d1, SIDE), lax.rem(self.y + d2, SIDE))

    def copy(self, h, e1, e2, f1, f2):
        r = self.src(h, e1, e2)
        k = (h, (e1 - f1) % SIDE, (e2 - f2) % SIDE)
        i = len(self.started)
        return remote(self.part(h, r), self.part(h, r), self.send.at[i], self.recv.at[k[0], k[1], k[2]],
                      "row", self.src(h, f1, f2))

    def begin(self, c):
        c.start()
        self.started.append(c)

    def first(self):
        for d in (1, 3, 2):
            for h in (0, 1):
                self.begin(self.copy(h, 0, 0, d, 0))
        self.forward(0)

    def forward(self, e):
        for d in (1, 3, 2):
            for h in (0, 1):
                self.begin(self.copy(h, e, 0, 0, d))

    def wait(self, e1, e2):
        for h in (0, 1):
            r = self.src(h, e1, e2)
            remote(self.part(h, r), self.part(h, r), self.send.at[0], self.recv.at[h, e1, e2], "row",
                   self.coord(h, 1)).wait_recv()

    def finish(self):
        for c in self.started:
            c.wait_send()


def kernel(lens_ref, owners_ref, act_h, grad_h, pin_h, pout_h, curv_h, store_h, out_ref,
           act, grad, pin, pout, curv, store, acc, spread, feats, pres, score, parts,
           in_sem, send1, recv1, send2, recv2, send3, recv3):
    mods, rows = lax.axis_size("mod"), lax.axis_size("row")
    mod_id, row_id = lax.axis_index("mod"), lax.axis_index("row")
    x, y = row_id // SIDE, lax.rem(row_id, SIDE)
    tokens, width = act.shape
    rank = pin.shape[0]
    queries = lens_ref.shape[1]
    tile = tokens // TILES

    copies = {}
    def fetch(name, src, dst, i):
        copies[name] = pltpu.make_async_copy(src, dst, in_sem.at[i])
        copies[name].start()
    fetch("pin", pin_h.at[0], pin, 0)
    fetch("act0", act_h.at[0, pl.ds(0, tile)], act.at[pl.ds(0, tile)], 1)
    fetch("pout", pout_h.at[0], pout, 2)
    fetch("grad0", grad_h.at[0, pl.ds(0, tile)], grad.at[pl.ds(0, tile)], 3)
    for t in range(1, TILES):
        at = pl.ds(t * tile, tile)
        fetch(f"act{t}", act_h.at[0, at], act.at[at], 2 + 2 * t)
        fetch(f"grad{t}", grad_h.at[0, at], grad.at[at], 3 + 2 * t)
    fetch("curv", curv_h.at[0], curv, 2 + 2 * TILES)
    fetch("store", store_h.at[0], store, 3 + 2 * TILES)

    barrier = pltpu.get_barrier_semaphore()
    for d in range(1, rows):
        pl.semaphore_signal(barrier, inc=1, device_id={"row": lax.rem(row_id + d, rows)}, device_id_type=pl.DeviceIdType.MESH)
    for d in range(1, mods):
        pl.semaphore_signal(barrier, inc=1, device_id={"mod": lax.rem(mod_id + d, mods)}, device_id_type=pl.DeviceIdType.MESH)

    i0 = lax.broadcasted_iota(jnp.int32, (queries, queries), 0)
    i1 = lax.broadcasted_iota(jnp.int32, (queries, queries), 1)
    own_r = owners_ref[...]
    len_r = lens_ref[...]
    own_rb = jnp.broadcast_to(own_r, (queries, queries))
    len_rb = jnp.broadcast_to(len_r, (queries, queries))
    own_c = jnp.sum(jnp.where(i0 == i1, own_rb, 0), axis=1, keepdims=True)
    len_c = jnp.sum(jnp.where(i0 == i1, len_rb, 0), axis=1, keepdims=True)
    same = own_c == own_rb
    before_c = same & (i1 < i0)
    before_r = same & (i0 < i1)
    rank_c = jnp.sum(jnp.where(before_c, 1, 0), axis=1, keepdims=True)
    rank_r = jnp.sum(jnp.where(before_r, 1, 0), axis=0, keepdims=True)
    off_r = jnp.sum(jnp.where(before_r, jnp.broadcast_to(len_c, (queries, queries)), 0), axis=0, keepdims=True)
    s0 = lax.broadcasted_iota(jnp.int32, (CAP, queries), 0)
    chosen = (jnp.broadcast_to(rank_r, (CAP, queries)) == s0) & (jnp.broadcast_to(own_r, (CAP, queries)) == row_id)
    begin = jnp.sum(jnp.where(chosen, jnp.broadcast_to(off_r, (CAP, queries)), 0), axis=1, keepdims=True)
    count = jnp.sum(jnp.where(chosen, jnp.broadcast_to(len_r, (CAP, queries)), 0), axis=1, keepdims=True)
    end = begin + count
    slot_c = own_c * CAP + rank_c
    g1 = lax.broadcasted_iota(jnp.int32, (queries, rows * CAP), 1)
    placer = jnp.where(jnp.broadcast_to(slot_c, (queries, rows * CAP)) == g1, 1.0, 0.0).astype(bf16)

    fresh = [True] * CAP
    copies["pin"].wait()
    copies["pout"].wait()
    for t in range(TILES):
        at = pl.ds(t * tile, tile)
        copies[f"act{t}"].wait()
        fin = dot_nt(act[at, :], pin[...])
        copies[f"grad{t}"].wait()
        fout = dot_nt(grad[at, :], pout[...])
        in_hi, in_lo = halves(fin)
        right = jnp.concatenate([in_hi, in_lo, in_hi], axis=0)
        right = jnp.concatenate([right, right], axis=1)
        fout_t = fout.T
        pos = lax.broadcasted_iota(jnp.int32, (CAP, tile), 1) + t * tile
        member = (pos >= begin) & (pos < end)
        member = jnp.where(member, 1.0, 0.0)
        slots = [s for s in range(CAP) if LEN_MIN * s < (t + 1) * tile and LEN_MAX * (s + 1) > t * tile]
        for s in slots:
            w = fout_t * member[s:s + 1, :]
            w_hi, w_lo = halves(w)
            left = jnp.concatenate([w_hi, w_hi, w_lo], axis=1)
            g = dot_nn(left, right)
            if fresh[s]:
                acc[s] = g
                fresh[s] = False
            else:
                acc[s] = acc[s] + g
    lane = lax.broadcasted_iota(jnp.int32, (rank // 2, 2 * rank), 1)
    for s in range(CAP):
        even = acc[s, pl.ds(0, rank // 2, stride=2), :]
        odd = acc[s, pl.ds(1, rank // 2, stride=2), :]
        spread[:, s, :] = jnp.where(lane < rank, even, odd)
    for r in range(rank // 2):
        feats[row_id, :, r * 128:(r + 1) * 128] = spread[r].astype(bf16)

    pl.semaphore_wait(barrier, rows - 1 + mods - 1)

    half = rank * rank // 2
    g1_ = Gather(lambda h, r: feats.at[r, :, pl.ds(h * half, half)], send1, recv1, x, y)
    g1_.first()
    for d in (1, 3, 2):
        g1_.wait(d, 0)
        g1_.forward(d)
    for e2 in (1, 3, 2):
        for e1 in (0, 1, 3, 2):
            g1_.wait(e1, e2)

    copies["curv"].wait()
    whole = feats[...].reshape(rows * CAP, rank * rank)
    pre = dot_nt(whole, curv[...]).astype(bf16)
    pre = dot_nn(placer, pre).astype(bf16)
    pres[row_id] = pre

    hq = queries // 2
    g2_ = Gather(lambda h, r: pres.at[r, pl.ds(h * hq, hq)], send2, recv2, x, y)
    g2_.first()
    for d in (1, 3, 2):
        g2_.wait(d, 0)
        g2_.forward(d)
    for e2 in (1, 3, 2):
        for e1 in (0, 1, 3, 2):
            g2_.wait(e1, e2)

    copies["store"].wait()
    cols = pres.shape[2]
    total = None
    for j in range(rows):
        part = dot_nt(pres[j], store[:, j * cols:(j + 1) * cols])
        total = part if total is None else total + part
    score[...] = total.reshape(score.shape)
    parts[mod_id] = score[mod_id]
    sent = []
    for d in range(1, mods):
        peer = lax.rem(mod_id + d, mods)
        c = remote(score.at[peer], parts.at[mod_id], send3.at[d], recv3.at[d], "mod", peer)
        c.start()
        sent.append(c)
    for c in sent:
        c.wait()
    summed = parts[0]
    for m in range(1, mods):
        summed = summed + parts[m]
    out_ref[...] = summed
    g1_.finish()
    g2_.finish()


def on_device(activations, out_grads, in_projection, out_projection, inv_curvature, store_grads, lengths, owners):
    _, tokens, width = activations.shape
    rank = in_projection.shape[1]
    queries = lengths.shape[0]
    mods, rows = lax.axis_size("mod"), lax.axis_size("row")
    held, depth = store_grads.shape[1], store_grads.shape[2]
    share = inv_curvature.shape[1]
    hbm = pl.BlockSpec(memory_space=pl.ANY)
    vmem = pl.BlockSpec(memory_space=pltpu.VMEM)
    dma = pltpu.SemaphoreType.DMA
    return pl.pallas_call(
        kernel,
        out_shape=jax.ShapeDtypeStruct((queries // mods, held), f32),
        in_specs=[vmem, vmem] + [hbm] * 6,
        out_specs=vmem,
        scratch_shapes=[
            pltpu.VMEM((tokens, width), bf16),
            pltpu.VMEM((tokens, width), bf16),
            pltpu.VMEM((rank, width), bf16),
            pltpu.VMEM((rank, width), bf16),
            pltpu.VMEM((share, depth), bf16),
            pltpu.VMEM((held, depth), bf16),
            pltpu.VMEM((CAP, rank, 2 * rank), f32),
            pltpu.VMEM((rank // 2, CAP, 2 * rank), f32),
            pltpu.VMEM((rows, CAP, rank * rank), bf16),
            pltpu.VMEM((rows, queries, share), bf16),
            pltpu.VMEM((mods, queries // mods, held), f32),
            pltpu.VMEM((mods, queries // mods, held), f32),
            dma((4 + 2 * TILES,)),
            dma((30,)), dma((2, SIDE, SIDE)),
            dma((30,)), dma((2, SIDE, SIDE)),
            dma((mods,)), dma((mods,)),
        ],
        compiler_params=pltpu.CompilerParams(collective_id=0, has_side_effects=True, vmem_limit_bytes=60 * 1024 * 1024),
    )(lengths.reshape(1, queries), owners.reshape(1, queries), activations, out_grads, in_projection,
      out_projection, inv_curvature, store_grads)


def solution(mesh):
    return jax.shard_map(
        on_device,
        mesh=mesh,
        in_specs=(
            P("mod", "row", None),
            P("mod", "row", None),
            P("mod", None, None),
            P("mod", None, None),
            P("mod", "row", None),
            P("mod", "row", None),
            P(),
            P(),
        ),
        out_specs=P("mod", "row"),
        check_vma=False,
    )
```

```python
import jax
import jax.numpy as jnp
from jax import lax
from jax.experimental import pallas as pl
from jax.experimental.pallas import tpu as pltpu
from jax.sharding import PartitionSpec as P

f32, bf16 = jnp.float32, jnp.bfloat16
CAP = 8
LEN_MAX, LEN_MIN = 128, 64
TILES = 4
PAIR = CAP // TILES
SIDE = 4


def dot_nt(a, b):
    return lax.dot_general(a, b, (((1,), (1,)), ((), ())), preferred_element_type=f32)


def dot_nn(a, b):
    return lax.dot_general(a, b, (((1,), (0,)), ((), ())), preferred_element_type=f32)


def halves(x):
    hi = x.astype(bf16)
    return hi, (x - hi.astype(f32)).astype(bf16)


def remote(src, dst, send, recv, axis, peer):
    return pltpu.make_async_remote_copy(
        src_ref=src, dst_ref=dst, send_sem=send, recv_sem=recv,
        device_id={axis: peer}, device_id_type=pl.DeviceIdType.MESH,
    )


def taken(ref, sem):
    pltpu.make_async_copy(ref, ref, sem).wait()


class Gather:
    def __init__(self, own, part, blocks, sems, x, y):
        self.own, self.part, self.blocks, self.x, self.y = own, part, blocks, x, y
        self.send, self.near, self.far, self.rest = (sems.at[i] for i in range(4))

    def at(self, h, d1, d2):
        dx, dy = (d2, d1) if h == 0 else (d1, d2)
        return lax.rem(self.x + dx, SIDE) * SIDE + lax.rem(self.y + dy, SIDE)

    def first(self):
        for d, sem in ((1, self.near), (3, self.near), (2, self.far)):
            for h in (0, 1):
                place = self.part(h, self.at(h, 0, 0))
                remote(self.own(h), place, self.send, sem, "row", self.at(h, d, 0)).start()
        for h in (0, 1):
            self.onward(h, 0, self.own(h))

    def onward(self, h, e, block):
        place = self.part(h, self.at(h, e, 0))

        def to(d, _):
            remote(block, place, self.send, self.rest, "row", self.at(h, 0, d)).start()
            return 0
        lax.fori_loop(1, SIDE, to, 0)

    def forward(self):
        taken(self.blocks(2), self.near)
        for h in (0, 1):
            for e in (1, 3):
                self.onward(h, e, self.part(h, self.at(h, e, 0)))
        taken(self.blocks(1), self.far)
        for h in (0, 1):
            self.onward(h, 2, self.part(h, self.at(h, 2, 0)))

    def wait(self):
        taken(self.blocks(12), self.rest)

    def finish(self):
        taken(self.blocks(15), self.send)


class Direct:
    def __init__(self, own, part, blocks, send, recv, x, y):
        self.own, self.part, self.blocks, self.send, self.recv, self.x, self.y = own, part, blocks, send, recv, x, y

    def first(self):
        def step(i, _):
            dx, dy = i // SIDE, lax.rem(i, SIDE)
            remote(self.own, self.part, self.send, self.recv.at[lax.rem(SIDE - dx, SIDE)], "row",
                   lax.rem(self.x + dx, SIDE) * SIDE + lax.rem(self.y + dy, SIDE)).start()
            return 0
        lax.fori_loop(1, SIDE * SIDE, step, 0)

    def wait_x(self, dx):
        @pl.when(dx == 0)
        def _():
            taken(self.blocks(SIDE - 1), self.recv.at[0])

        @pl.when(dx != 0)
        def _():
            taken(self.blocks(SIDE), self.recv.at[dx])

    def finish(self):
        taken(self.blocks(SIDE * SIDE - 1), self.send)


def kernel(lens_h, owners_h, act_h, grad_h, pin_h, pout_h, curv_h, store_h, out_ref,
           lens, owners, rowsv, proj, curv, store, res, limits, acc, spread, ready, feats, pres, total, score, parts,
           in_sem, own_sem, sems1, sems2, last1, last2, sems3):
    mods, rows = lax.axis_size("mod"), lax.axis_size("row")
    mod_id, row_id = lax.axis_index("mod"), lax.axis_index("row")
    x, y = row_id // SIDE, lax.rem(row_id, SIDE)
    tokens, width = rowsv.shape[1:]
    rank = proj.shape[1]
    entries = rank * rank
    queries = lens_h.shape[1]
    share = curv.shape[0]
    tile = tokens // TILES

    tile_sem, proj_sem, late_sem, small_sem = in_sem
    small = [pltpu.make_async_copy(lens_h, lens, small_sem.at[0]), pltpu.make_async_copy(owners_h, owners, small_sem.at[1])]
    projs = [pltpu.make_async_copy(h.at[0], proj.at[m], proj_sem.at[m]) for m, h in enumerate((pin_h, pout_h))]
    late = [pltpu.make_async_copy(curv_h.at[0], curv, late_sem.at[0]), pltpu.make_async_copy(store_h.at[0], store, late_sem.at[1])]

    def tile_copy(m, t):
        at = pl.ds(pl.multiple_of(t * tile, tile), tile)
        return pltpu.make_async_copy((act_h, grad_h)[m].at[0, at], rowsv.at[m, at], tile_sem.at[m, t])

    small[0].start()
    small[1].start()
    for m in (0, 1):
        projs[m].start()
        tile_copy(m, 0).start()

    def fetch_tile(t, _):
        tile_copy(0, t).start()
        tile_copy(1, t).start()
        return 0
    lax.fori_loop(1, TILES, fetch_tile, 0)

    barrier = pltpu.get_barrier_semaphore()

    def greet(axis, me, n):
        def step(d, _):
            pl.semaphore_signal(barrier, inc=1, device_id={axis: lax.rem(me + d, n)}, device_id_type=pl.DeviceIdType.MESH)
            return 0
        lax.fori_loop(1, n, step, 0)
    greet("row", row_id, rows)
    greet("mod", mod_id, mods)

    small[0].wait()
    small[1].wait()
    i0 = lax.broadcasted_iota(jnp.int32, (queries, queries), 0)
    i1 = lax.broadcasted_iota(jnp.int32, (queries, queries), 1)
    own_r = owners[...]
    len_r = lens[...]
    own_rb = jnp.broadcast_to(own_r, (queries, queries))
    len_rb = jnp.broadcast_to(len_r, (queries, queries))
    own_c = jnp.sum(jnp.where(i0 == i1, own_rb, 0), axis=1, keepdims=True)
    len_c = jnp.sum(jnp.where(i0 == i1, len_rb, 0), axis=1, keepdims=True)
    same = own_c == own_rb
    before_c = same & (i1 < i0)
    before_r = same & (i0 < i1)
    rank_c = jnp.sum(jnp.where(before_c, 1, 0), axis=1, keepdims=True)
    rank_r = jnp.sum(jnp.where(before_r, 1, 0), axis=0, keepdims=True)
    off_r = jnp.sum(jnp.where(before_r, jnp.broadcast_to(len_c, (queries, queries)), 0), axis=0, keepdims=True)
    s0 = lax.broadcasted_iota(jnp.int32, (CAP, queries), 0)
    chosen = (jnp.broadcast_to(rank_r, (CAP, queries)) == s0) & (jnp.broadcast_to(own_r, (CAP, queries)) == row_id)
    begin = jnp.sum(jnp.where(chosen, jnp.broadcast_to(off_r, (CAP, queries)), 0), axis=1, keepdims=True)
    count = jnp.sum(jnp.where(chosen, jnp.broadcast_to(len_r, (CAP, queries)), 0), axis=1, keepdims=True)
    limits[0] = jnp.broadcast_to(begin, limits.shape[1:])
    limits[1] = jnp.broadcast_to(begin + count, limits.shape[1:])
    slot_c = (rank_c // PAIR) * (rows * PAIR) + own_c * PAIR + rank_c % PAIR

    def row_pair(r):
        return pl.ds(pl.multiple_of(r * PAIR, PAIR), PAIR)

    LAST = TILES - 1

    def features(t):
        half = entries // 2
        return Gather(lambda h: ready.at[t, pl.ds(0, PAIR), pl.ds(h * half, half)],
                      lambda h, r: feats.at[t, row_pair(r), pl.ds(h * half, half)],
                      lambda n: pres.at[t, pl.ds(0, n)], sems1.at[t], x, y)

    last_features = Direct(ready.at[LAST, pl.ds(0, PAIR)], feats.at[LAST, row_pair(row_id)],
                           lambda n: pres.at[LAST, pl.ds(0, n)], last1.at[SIDE], last1, x, y)

    def pre_rows(t):
        half = rows * PAIR // 2
        return Gather(lambda h: pres.at[t, row_id, pl.ds(h * half, half)],
                      lambda h, r: pres.at[t, r, pl.ds(h * half, half)],
                      lambda n: pres.at[t, pl.ds(0, n)], sems2.at[t], x, y)

    last_pre_rows = Direct(pres.at[LAST, row_id], pres.at[LAST, row_id],
                           lambda n: pres.at[LAST, pl.ds(0, n)], last2.at[SIDE], last2, x, y)

    def own(t):
        return pltpu.make_async_copy(ready.at[t, pl.ds(0, PAIR)], feats.at[t, row_pair(row_id)], own_sem.at[t])

    acc[...] = jnp.zeros_like(acc)
    projs[0].wait()
    projs[1].wait()

    def token_tile(t, _):
        at = pl.ds(pl.multiple_of(t * tile, tile), tile)

        def side(m, _):
            pltpu.make_async_copy(act_h.at[0, at], rowsv.at[m, at], tile_sem.at[m, t]).wait()
            res[m] = dot_nt(rowsv[m, at, :], proj[m])
            return 0
        lax.fori_loop(0, 2, side, 0)

        @pl.when(t == 1)
        def _():
            late[0].start()
            late[1].start()

        in_hi, in_lo = halves(res[0])
        in_hi = jnp.concatenate([in_hi, in_hi], axis=1)
        in_lo = jnp.concatenate([in_lo, in_lo], axis=1)
        right = jnp.concatenate([jnp.concatenate([in_hi, in_lo], axis=1)] * 2, axis=0)
        fout_t = res[1].T
        pos = lax.broadcasted_iota(jnp.int32, (CAP, tile), 1) + t * tile
        member = jnp.where((pos >= limits[0]) & (pos < limits[1]), 1.0, 0.0)
        member = member.astype(bf16)
        out_hi, out_lo = halves(fout_t)
        left = []
        for s in range(CAP):
            m = jnp.broadcast_to(member[s:s + 1, :], out_hi.shape)
            left.append(jnp.concatenate([out_hi * m, out_lo * m], axis=1))
        g = dot_nn(jnp.concatenate(left, axis=0), right)
        acc[...] = acc[...] + (g[:, :2 * rank] + g[:, 2 * rank:])
        lane = lax.broadcasted_iota(jnp.int32, (rank // 2, 2 * rank), 1)
        for p in range(PAIR):
            base = pl.multiple_of((t * PAIR + p) * rank, rank)
            even = acc[pl.ds(base, rank // 2, stride=2), :]
            odd = acc[pl.ds(base + 1, rank // 2, stride=2), :]
            spread[:, p, :] = jnp.where(lane < rank, even, odd)
        for r in range(rank // 2):
            ready[t, 0:PAIR, r * 128:(r + 1) * 128] = spread[r, 0:PAIR, :].astype(bf16)

        @pl.when(t == 0)
        def _():
            pl.semaphore_wait(barrier, rows - 1 + mods - 1)
        own(t).start()

        @pl.when(t != LAST)
        def _():
            features(t).first()

        @pl.when(t == LAST)
        def _():
            last_features.first()

        @pl.when(t >= 2)
        def _():
            features(t - 2).forward()
        return 0
    lax.fori_loop(0, TILES, token_tile, 0)

    late[0].wait()

    def precondition(t):
        own(t).wait()
        chunk = 4 * share

        def step(k, sums):
            at = pl.ds(pl.multiple_of(k * chunk, chunk), chunk)
            return sums + dot_nt(feats[t, :, at], curv[:, at])
        sums = lax.fori_loop(0, entries // chunk, step, jnp.zeros((rows * PAIR, share), f32))
        pres[t, row_id] = sums.astype(bf16)

    def batch(t, _):
        @pl.when(t == 1)
        def _():
            features(2).forward()

        features(t).wait()
        precondition(t)
        pre_rows(t).first()

        @pl.when(t >= 1)
        def _():
            pre_rows(t - 1).forward()
        return 0
    lax.fori_loop(0, LAST, batch, 0)

    def arrived(dx, _):
        last_features.wait_x(dx)
        return 0
    lax.fori_loop(0, SIDE, arrived, 0)
    precondition(LAST)
    last_pre_rows.first()
    pre_rows(LAST - 1).forward()

    late[1].wait()
    total[...] = jnp.zeros_like(total)

    def here(t, _):
        pre_rows(t).wait()
        return 0
    lax.fori_loop(0, LAST, here, 0)

    def source(dx, _):
        last_pre_rows.wait_x(dx)
        r = lax.rem(x + dx, SIDE) * SIDE
        left = [jnp.concatenate([pres[t, r + k] for t in range(TILES)], axis=0) for k in range(SIDE)]
        right = store[:, pl.ds(pl.multiple_of(r * share, SIDE * share), SIDE * share)]
        total[...] = total[...] + dot_nt(jnp.concatenate(left, axis=1), right)
        return 0
    lax.fori_loop(0, SIDE, source, 0)

    g1 = lax.broadcasted_iota(jnp.int32, (queries, rows * CAP), 1)
    placer = jnp.where(jnp.broadcast_to(slot_c, (queries, rows * CAP)) == g1, 1.0, 0.0).astype(bf16)
    score[...] = dot_nn(placer, total[...].astype(bf16)).astype(bf16).reshape(score.shape)

    def send(d, _):
        peer = lax.rem(mod_id + d, mods)
        remote(score.at[peer], parts.at[mod_id], sems3.at[0], sems3.at[1], "mod", peer).start()
        return 0
    lax.fori_loop(1, mods, send, 0)
    parts[mod_id] = score[mod_id]
    taken(parts.at[pl.ds(0, mods - 1)], sems3.at[1])
    summed = parts[0].astype(f32)
    for m in range(1, mods):
        summed = summed + parts[m].astype(f32)
    out_ref[...] = summed

    def finish(t, _):
        features(t).finish()
        pre_rows(t).finish()
        return 0
    lax.fori_loop(0, LAST, finish, 0)
    last_features.finish()
    last_pre_rows.finish()
    taken(score.at[pl.ds(0, mods - 1)], sems3.at[0])


def on_device(activations, out_grads, in_projection, out_projection, inv_curvature, store_grads, lengths, owners):
    _, tokens, width = activations.shape
    rank = in_projection.shape[1]
    queries = lengths.shape[0]
    mods, rows = lax.axis_size("mod"), lax.axis_size("row")
    held, depth = store_grads.shape[1], store_grads.shape[2]
    share = inv_curvature.shape[1]
    hbm = pl.BlockSpec(memory_space=pl.ANY)
    vmem = pl.BlockSpec(memory_space=pltpu.VMEM)
    dma = pltpu.SemaphoreType.DMA
    return pl.pallas_call(
        kernel,
        out_shape=jax.ShapeDtypeStruct((queries // mods, held), f32),
        in_specs=[hbm] * 8,
        out_specs=vmem,
        scratch_shapes=[
            pltpu.VMEM((1, queries), jnp.int32),
            pltpu.VMEM((1, queries), jnp.int32),
            pltpu.VMEM((2, tokens, width), bf16),
            pltpu.VMEM((2, rank, width), bf16),
            pltpu.VMEM((share, depth), bf16),
            pltpu.VMEM((held, depth), bf16),
            pltpu.VMEM((2, tokens // TILES, rank), f32),
            pltpu.VMEM((2, CAP, tokens // TILES), jnp.int32),
            pltpu.VMEM((CAP * rank, 2 * rank), f32),
            pltpu.VMEM((rank // 2, CAP, 2 * rank), f32),
            pltpu.VMEM((TILES, CAP, rank * rank), bf16),
            pltpu.VMEM((TILES, rows * PAIR, rank * rank), bf16),
            pltpu.VMEM((TILES, rows, rows * PAIR, share), bf16),
            pltpu.VMEM((rows * CAP, held), f32),
            pltpu.VMEM((mods, queries // mods, held), bf16),
            pltpu.VMEM((mods, queries // mods, held), bf16),
            (dma((2, TILES)), dma((2,)), dma((2,)), dma((2,))),
            dma((TILES,)),
            dma((TILES - 1, 4)), dma((TILES - 1, 4)),
            dma((SIDE + 1,)), dma((SIDE + 1,)),
            dma((2,)),
        ],
        compiler_params=pltpu.CompilerParams(collective_id=0, has_side_effects=True, vmem_limit_bytes=60 * 1024 * 1024),
    )(lengths.reshape(1, queries), owners.reshape(1, queries), activations, out_grads, in_projection,
      out_projection, inv_curvature, store_grads)


def solution(mesh):
    return jax.shard_map(
        on_device,
        mesh=mesh,
        in_specs=(
            P("mod", "row", None),
            P("mod", "row", None),
            P("mod", None, None),
            P("mod", None, None),
            P("mod", "row", None),
            P("mod", "row", None),
            P(),
            P(),
        ),
        out_specs=P("mod", "row"),
        check_vma=False,
    )
```

```python
import jax
import jax.numpy as jnp
from jax import lax
from jax.experimental import pallas as pl
from jax.experimental.pallas import tpu as pltpu
from jax.sharding import PartitionSpec as P

f32, bf16 = jnp.float32, jnp.bfloat16
CAP = 8
LEN_MAX, LEN_MIN = 128, 64
TILES = 4
RELAYED = 1
PAIR = CAP // TILES
SIDE = 4
FAR_FIRST = sorted(((dx, dy) for dx in range(SIDE) for dy in range(SIDE) if dx or dy),
                   key=lambda d: -sum(min(c, SIDE - c) for c in d))


def dot_nt(a, b):
    return lax.dot_general(a, b, (((1,), (1,)), ((), ())), preferred_element_type=f32)


def dot_nn(a, b):
    return lax.dot_general(a, b, (((1,), (0,)), ((), ())), preferred_element_type=f32)


def halves(x):
    hi = x.astype(bf16)
    return hi, (x - hi.astype(f32)).astype(bf16)


def remote(src, dst, send, recv, axis, peer):
    return pltpu.make_async_remote_copy(
        src_ref=src, dst_ref=dst, send_sem=send, recv_sem=recv,
        device_id={axis: peer}, device_id_type=pl.DeviceIdType.MESH,
    )


def taken(ref, sem):
    pltpu.make_async_copy(ref, ref, sem).wait()


class Gather:
    def __init__(self, own, part, blocks, sems, x, y):
        self.own, self.part, self.blocks, self.x, self.y = own, part, blocks, x, y
        self.send, self.near, self.far, self.rest = (sems.at[i] for i in range(4))

    def at(self, h, d1, d2):
        dx, dy = (d2, d1) if h == 0 else (d1, d2)
        return lax.rem(self.x + dx, SIDE) * SIDE + lax.rem(self.y + dy, SIDE)

    def first(self):
        for d, sem in ((1, self.near), (3, self.near), (2, self.far)):
            for h in (0, 1):
                place = self.part(h, self.at(h, 0, 0))
                remote(self.own(h), place, self.send, sem, "row", self.at(h, d, 0)).start()
        for h in (0, 1):
            self.onward(h, 0, self.own(h))

    def onward(self, h, e, block):
        place = self.part(h, self.at(h, e, 0))

        def to(d, _):
            remote(block, place, self.send, self.rest, "row", self.at(h, 0, d)).start()
            return 0
        lax.fori_loop(1, SIDE, to, 0)

    def forward_near(self):
        taken(self.blocks(2), self.near)
        for h in (0, 1):
            for e in (1, 3):
                self.onward(h, e, self.part(h, self.at(h, e, 0)))

    def forward_far(self):
        taken(self.blocks(1), self.far)
        for h in (0, 1):
            self.onward(h, 2, self.part(h, self.at(h, 2, 0)))

    def wait(self):
        taken(self.blocks(12), self.rest)

    def finish(self):
        taken(self.blocks(15), self.send)


class Direct:
    def __init__(self, own, part, blocks, send, recv, x, y):
        self.own, self.part, self.blocks, self.send, self.recv, self.x, self.y = own, part, blocks, send, recv, x, y

    def first(self):
        for dx, dy in FAR_FIRST:
            recv = self.recv.at[(SIDE - dx) % SIDE] if len(self.recv.shape) else self.recv
            remote(self.own, self.part, self.send, recv, "row",
                   lax.rem(self.x + dx, SIDE) * SIDE + lax.rem(self.y + dy, SIDE)).start()

    def wait(self):
        taken(self.blocks(SIDE * SIDE - 1), self.recv)

    def wait_x(self, dx):
        @pl.when(dx == 0)
        def _():
            taken(self.blocks(SIDE - 1), self.recv.at[0])

        @pl.when(dx != 0)
        def _():
            taken(self.blocks(SIDE), self.recv.at[dx])

    def finish(self):
        taken(self.blocks(SIDE * SIDE - 1), self.send)


def kernel(lens_h, owners_h, act_h, grad_h, pin_h, pout_h, curv_h, store_h, out_ref,
           lens, owners, rowsv, proj, curv, store, res, limits, acc, spread, ready, feats, pres, last_pres, late_hot, final_hot, total, score, parts,
           in_sem, own_sem, sems1, sems2, last1, last2, sems3):
    mods, rows = lax.axis_size("mod"), lax.axis_size("row")
    mod_id, row_id = lax.axis_index("mod"), lax.axis_index("row")
    x, y = row_id // SIDE, lax.rem(row_id, SIDE)
    tokens, width = rowsv.shape[1:]
    rank = proj.shape[1]
    entries = rank * rank
    queries = lens_h.shape[1]
    share = curv.shape[0]
    tile = tokens // TILES
    LAST = TILES - 1

    tile_sem, proj_sem, late_sem, small_sem = in_sem
    small = [pltpu.make_async_copy(lens_h, lens, small_sem.at[0]), pltpu.make_async_copy(owners_h, owners, small_sem.at[1])]
    projs = [pltpu.make_async_copy(h.at[0], proj.at[m], proj_sem.at[m]) for m, h in enumerate((pin_h, pout_h))]
    late = [pltpu.make_async_copy(curv_h.at[0], curv, late_sem.at[0]), pltpu.make_async_copy(store_h.at[0], store, late_sem.at[1])]

    def tile_copy(m, t):
        at = pl.ds(pl.multiple_of(t * tile, tile), tile)
        return pltpu.make_async_copy((act_h, grad_h)[m].at[0, at], rowsv.at[m, at], tile_sem.at[m, t])

    small[0].start()
    small[1].start()
    for m in (0, 1):
        projs[m].start()
        tile_copy(m, 0).start()

    def fetch_tile(t, _):
        tile_copy(0, t).start()
        tile_copy(1, t).start()
        return 0
    lax.fori_loop(1, TILES, fetch_tile, 0)

    barrier = pltpu.get_barrier_semaphore()

    def greet(axis, me, n):
        def step(d, _):
            pl.semaphore_signal(barrier, inc=1, device_id={axis: lax.rem(me + d, n)}, device_id_type=pl.DeviceIdType.MESH)
            return 0
        lax.fori_loop(1, n, step, 0)
    greet("row", row_id, rows)
    greet("mod", mod_id, mods)

    small[0].wait()
    small[1].wait()
    i0 = lax.broadcasted_iota(jnp.int32, (queries, queries), 0)
    i1 = lax.broadcasted_iota(jnp.int32, (queries, queries), 1)
    own_r = owners[...]
    len_r = lens[...]
    own_rb = jnp.broadcast_to(own_r, (queries, queries))
    len_rb = jnp.broadcast_to(len_r, (queries, queries))
    own_c = jnp.sum(jnp.where(i0 == i1, own_rb, 0), axis=1, keepdims=True)
    len_c = jnp.sum(jnp.where(i0 == i1, len_rb, 0), axis=1, keepdims=True)
    same = own_c == own_rb
    before_c = same & (i1 < i0)
    before_r = same & (i0 < i1)
    rank_c = jnp.sum(jnp.where(before_c, 1, 0), axis=1, keepdims=True)
    rank_r = jnp.sum(jnp.where(before_r, 1, 0), axis=0, keepdims=True)
    off_r = jnp.sum(jnp.where(before_r, jnp.broadcast_to(len_c, (queries, queries)), 0), axis=0, keepdims=True)
    s0 = lax.broadcasted_iota(jnp.int32, (CAP, queries), 0)
    chosen = (jnp.broadcast_to(rank_r, (CAP, queries)) == s0) & (jnp.broadcast_to(own_r, (CAP, queries)) == row_id)
    begin = jnp.sum(jnp.where(chosen, jnp.broadcast_to(off_r, (CAP, queries)), 0), axis=1, keepdims=True)
    count = jnp.sum(jnp.where(chosen, jnp.broadcast_to(len_r, (CAP, queries)), 0), axis=1, keepdims=True)
    limits[0] = jnp.broadcast_to(begin, limits.shape[1:])
    limits[1] = jnp.broadcast_to(begin + count, limits.shape[1:])
    slot_c = (rank_c // PAIR) * (rows * PAIR) + own_c * PAIR + rank_c % PAIR
    early_rows = late_rows = rows * CAP // 2
    late_most = queries // 2
    is_late_r, is_late_c = rank_r >= CAP // 2, rank_c >= CAP // 2
    place_c = jnp.sum(jnp.where((i1 < i0) & jnp.broadcast_to(is_late_r, (queries, queries)), 1, 0), axis=1, keepdims=True)
    place_r = jnp.sum(jnp.where((i0 < i1) & jnp.broadcast_to(is_late_c, (queries, queries)), 1, 0), axis=0, keepdims=True)
    place_c = jnp.where(is_late_c, place_c, -1)
    place_r = jnp.where(is_late_r, place_r, -1)

    def one_hot(left, right):
        return jnp.where(left == right, 1.0, 0.0).astype(bf16)

    def along(n, m, axis):
        return lax.broadcasted_iota(jnp.int32, (n, m), axis)

    pick = one_hot(jnp.broadcast_to(place_r, (late_most, queries)), along(late_most, queries, 0))
    slots_hot = one_hot(jnp.broadcast_to(slot_c, (queries, late_rows)), along(queries, late_rows, 1) + early_rows)
    late_hot[...] = dot_nn(pick, slots_hot).astype(bf16)
    final_c = jnp.where(is_late_c, place_c + early_rows, slot_c)
    final_hot[...] = one_hot(jnp.broadcast_to(final_c, final_hot.shape), along(*final_hot.shape, 1))

    def row_pair(r):
        return pl.ds(pl.multiple_of(r * PAIR, PAIR), PAIR)

    def ready_like(n):
        return pres.at[pl.ds(0, n), pl.ds(0, queries // 2)]

    def features(t):
        half = entries // 2
        return Gather(lambda h: ready.at[t, pl.ds(0, PAIR), pl.ds(h * half, half)],
                      lambda h, r: feats.at[t, row_pair(r), pl.ds(h * half, half)],
                      lambda n: ready_like(n), sems1.at[t], x, y)

    def straight(t):
        return Direct(ready.at[t, pl.ds(0, PAIR)], feats.at[t, row_pair(row_id)], ready_like, last1.at[t - RELAYED, 1],
                      last1.at[t - RELAYED, 0], x, y)

    early_half = rows * CAP // 4
    pre_rows = Gather(lambda h: pres.at[row_id, pl.ds(h * early_half, early_half)],
                      lambda h, r: pres.at[r, pl.ds(h * early_half, early_half)],
                      lambda n: pres.at[pl.ds(0, n)], sems2, x, y)
    last_pre_rows = Direct(last_pres.at[row_id], last_pres.at[row_id],
                           lambda n: last_pres.at[pl.ds(0, n)], last2.at[SIDE], last2, x, y)

    def own(t):
        return pltpu.make_async_copy(ready.at[t, pl.ds(0, PAIR)], feats.at[t, row_pair(row_id)], own_sem.at[t])

    acc[...] = jnp.zeros_like(acc)
    projs[0].wait()
    projs[1].wait()

    def token_tile(t, _):
        at = pl.ds(pl.multiple_of(t * tile, tile), tile)

        def side(m, _):
            pltpu.make_async_copy(act_h.at[0, at], rowsv.at[m, at], tile_sem.at[m, t]).wait()
            res[m] = dot_nt(rowsv[m, at, :], proj[m])
            return 0
        lax.fori_loop(0, 2, side, 0)

        @pl.when(t == 1)
        def _():
            late[0].start()
            late[1].start()

        @pl.when(t == 0)
        def _():
            pl.semaphore_wait(barrier, rows - 1 + mods - 1)

        @pl.when((t >= 2) & (t <= RELAYED + 1))
        def _():
            features(t - 2).forward_far()

        in_hi, in_lo = halves(res[0])
        in_hi = jnp.concatenate([in_hi, in_hi], axis=1)
        in_lo = jnp.concatenate([in_lo, in_lo], axis=1)
        right = jnp.concatenate([jnp.concatenate([in_hi, in_lo], axis=1)] * 2, axis=0)
        fout_t = res[1].T
        pos = lax.broadcasted_iota(jnp.int32, (CAP, tile), 1) + t * tile
        member = jnp.where((pos >= limits[0]) & (pos < limits[1]), 1.0, 0.0)
        member = member.astype(bf16)
        out_hi, out_lo = halves(fout_t)
        left = []
        for s in range(CAP):
            m = jnp.broadcast_to(member[s:s + 1, :], out_hi.shape)
            left.append(jnp.concatenate([out_hi * m, out_lo * m], axis=1))
        g = dot_nn(jnp.concatenate(left, axis=0), right)
        acc[...] = acc[...] + (g[:, :2 * rank] + g[:, 2 * rank:])
        lane = lax.broadcasted_iota(jnp.int32, (rank // 2, 2 * rank), 1)
        for p in range(PAIR):
            base = pl.multiple_of((t * PAIR + p) * rank, rank)
            even = acc[pl.ds(base, rank // 2, stride=2), :]
            odd = acc[pl.ds(base + 1, rank // 2, stride=2), :]
            spread[:, p, :] = jnp.where(lane < rank, even, odd)
        for r in range(rank // 2):
            ready[t, 0:PAIR, r * 128:(r + 1) * 128] = spread[r, 0:PAIR, :].astype(bf16)

        own(t).start()

        @pl.when(t < RELAYED)
        def _():
            features(t).first()

        @pl.when(t >= RELAYED)
        def _():
            straight(t).first()

        @pl.when((t >= 1) & (t <= RELAYED))
        def _():
            features(t - 1).forward_near()
        return 0
    lax.fori_loop(0, TILES, token_tile, 0)

    late[0].wait()

    chunk = 16 * share

    def precondition(ts):
        def step(k, sums):
            at = pl.ds(pl.multiple_of(k * chunk, chunk), chunk)
            return sums + dot_nt(jnp.concatenate([feats[t, :, at] for t in ts], axis=0), curv[:, at])
        sums = lax.fori_loop(0, entries // chunk, step, jnp.zeros((len(ts) * rows * PAIR, share), f32))
        return sums.astype(bf16)

    def turned(ts):
        def step(k, sums):
            at = pl.ds(pl.multiple_of(k * chunk, chunk), chunk)
            return sums + dot_nt(curv[:, at], jnp.concatenate([feats[t, :, at] for t in ts], axis=0))
        sums = lax.fori_loop(0, entries // chunk, step, jnp.zeros((share, len(ts) * rows * PAIR), f32))
        return sums.astype(bf16)

    for t in range(2):
        (features(t) if t < RELAYED else straight(t)).wait()
        own(t).wait()
    pres[row_id] = precondition((0, 1))
    pre_rows.first()
    straight(2).wait()
    own(2).wait()
    pre_rows.forward_near()
    pre_rows.forward_far()
    straight(LAST).wait()
    own(LAST).wait()
    last_pres[row_id] = dot_nt(late_hot[...], turned((2, LAST))).astype(bf16)
    last_pre_rows.first()

    late[1].wait()
    total[...] = jnp.zeros_like(total)
    pre_rows.wait()

    def source(dx, _):
        last_pre_rows.wait_x(dx)
        r = lax.rem(x + dx, SIDE) * SIDE
        left = [jnp.concatenate([pres[r + k], last_pres[r + k]], axis=0) for k in range(SIDE)]
        right = store[:, pl.ds(pl.multiple_of(r * share, SIDE * share), SIDE * share)]
        total[...] = total[...] + dot_nt(right, jnp.concatenate(left, axis=1))
        return 0
    for dx in range(SIDE):
        source(dx, 0)

    score[...] = dot_nt(final_hot[...], total[...].astype(bf16)).astype(bf16).reshape(score.shape)

    def send(d, _):
        peer = lax.rem(mod_id + d, mods)
        remote(score.at[peer], parts.at[mod_id], sems3.at[0], sems3.at[1], "mod", peer).start()
        return 0
    lax.fori_loop(1, mods, send, 0)
    parts[mod_id] = score[mod_id]
    for t in range(TILES):
        (features(t) if t < RELAYED else straight(t)).finish()
    pre_rows.finish()
    last_pre_rows.finish()
    taken(parts.at[pl.ds(0, mods - 1)], sems3.at[1])
    summed = parts[0].astype(f32)
    for m in range(1, mods):
        summed = summed + parts[m].astype(f32)
    out_ref[...] = summed

    taken(score.at[pl.ds(0, mods - 1)], sems3.at[0])


def on_device(activations, out_grads, in_projection, out_projection, inv_curvature, store_grads, lengths, owners):
    _, tokens, width = activations.shape
    rank = in_projection.shape[1]
    queries = lengths.shape[0]
    mods, rows = lax.axis_size("mod"), lax.axis_size("row")
    held, depth = store_grads.shape[1], store_grads.shape[2]
    share = inv_curvature.shape[1]
    hbm = pl.BlockSpec(memory_space=pl.ANY)
    vmem = pl.BlockSpec(memory_space=pltpu.VMEM)
    dma = pltpu.SemaphoreType.DMA
    return pl.pallas_call(
        kernel,
        out_shape=pltpu.VMEM((queries // mods, held), f32),
        in_specs=[hbm] * 8,
        out_specs=vmem,
        scratch_shapes=[
            pltpu.VMEM((1, queries), jnp.int32),
            pltpu.VMEM((1, queries), jnp.int32),
            pltpu.VMEM((2, tokens, width), bf16),
            pltpu.VMEM((2, rank, width), bf16),
            pltpu.VMEM((share, depth), bf16),
            pltpu.VMEM((held, depth), bf16),
            pltpu.VMEM((2, tokens // TILES, rank), f32),
            pltpu.VMEM((2, CAP, tokens // TILES), jnp.int32),
            pltpu.VMEM((CAP * rank, 2 * rank), f32),
            pltpu.VMEM((rank // 2, CAP, 2 * rank), f32),
            pltpu.VMEM((TILES, CAP, rank * rank), bf16),
            pltpu.VMEM((TILES, rows * PAIR, rank * rank), bf16),
            pltpu.VMEM((rows, rows * CAP // 2, share), bf16),
            pltpu.VMEM((rows, queries // 2, share), bf16),
            pltpu.VMEM((queries // 2, rows * CAP // 2), bf16),
            pltpu.VMEM((queries, rows * CAP // 2 + queries // 2), bf16),
            pltpu.VMEM((held, rows * CAP // 2 + queries // 2), f32),
            pltpu.VMEM((mods, queries // mods, held), bf16),
            pltpu.VMEM((mods, queries // mods, held), bf16),
            (dma((2, TILES)), dma((2,)), dma((2,)), dma((2,))),
            dma((TILES,)),
            dma((max(RELAYED,1), 4)), dma((4,)),
            dma((TILES - RELAYED, 2)), dma((SIDE + 1,)),
            dma((2,)),
        ],
        compiler_params=pltpu.CompilerParams(collective_id=0, has_side_effects=True, vmem_limit_bytes=60 * 1024 * 1024),
    )(lengths.reshape(1, queries), owners.reshape(1, queries), activations, out_grads, in_projection,
      out_projection, inv_curvature, store_grads)


def solution(mesh):
    return jax.shard_map(
        on_device,
        mesh=mesh,
        in_specs=(
            P("mod", "row", None),
            P("mod", "row", None),
            P("mod", None, None),
            P("mod", None, None),
            P("mod", "row", None),
            P("mod", "row", None),
            P(),
            P(),
        ),
        out_specs=P("mod", "row"),
        check_vma=False,
    )
```

```python
import jax
import jax.numpy as jnp
from jax import lax
from jax.experimental import pallas as pl
from jax.experimental.pallas import tpu as pltpu
from jax.sharding import PartitionSpec as P

f32, bf16 = jnp.float32, jnp.bfloat16
CAP = 8
LEN_MAX, LEN_MIN = 128, 64
TILES = 4
RELAYED = 3
PAIR = CAP // TILES
SIDE = 4
FAR_FIRST = sorted(((dx, dy) for dx in range(SIDE) for dy in range(SIDE) if dx or dy),
                   key=lambda d: -sum(min(c, SIDE - c) for c in d))


def dot_nt(a, b):
    return lax.dot_general(a, b, (((1,), (1,)), ((), ())), preferred_element_type=f32)


def dot_nn(a, b):
    return lax.dot_general(a, b, (((1,), (0,)), ((), ())), preferred_element_type=f32)


def halves(x):
    hi = x.astype(bf16)
    return hi, (x - hi.astype(f32)).astype(bf16)


def remote(src, dst, send, recv, axis, peer):
    return pltpu.make_async_remote_copy(
        src_ref=src, dst_ref=dst, send_sem=send, recv_sem=recv,
        device_id={axis: peer}, device_id_type=pl.DeviceIdType.MESH,
    )


def taken(ref, sem):
    pltpu.make_async_copy(ref, ref, sem).wait()


class Gather:
    def __init__(self, own, part, blocks, sems, x, y):
        self.own, self.part, self.blocks, self.x, self.y = own, part, blocks, x, y
        self.send, self.near, self.far, self.rest = (sems.at[i] for i in range(4))

    def at(self, h, d1, d2):
        dx, dy = (d2, d1) if h == 0 else (d1, d2)
        return lax.rem(self.x + dx, SIDE) * SIDE + lax.rem(self.y + dy, SIDE)

    def first(self):
        for d, sem in ((1, self.near), (3, self.near), (2, self.far)):
            for h in (0, 1):
                place = self.part(h, self.at(h, 0, 0))
                remote(self.own(h), place, self.send, sem, "row", self.at(h, d, 0)).start()
        for h in (0, 1):
            self.onward(h, 0, self.own(h))

    def onward(self, h, e, block):
        place = self.part(h, self.at(h, e, 0))

        def to(d, _):
            remote(block, place, self.send, self.rest, "row", self.at(h, 0, d)).start()
            return 0
        lax.fori_loop(1, SIDE, to, 0)

    def forward_near(self):
        taken(self.blocks(2), self.near)
        for h in (0, 1):
            for e in (1, 3):
                self.onward(h, e, self.part(h, self.at(h, e, 0)))

    def forward_far(self):
        taken(self.blocks(1), self.far)
        for h in (0, 1):
            self.onward(h, 2, self.part(h, self.at(h, 2, 0)))

    def wait(self):
        taken(self.blocks(12), self.rest)

    def finish(self):
        taken(self.blocks(15), self.send)


class Direct:
    def __init__(self, own, part, blocks, send, recv, x, y):
        self.own, self.part, self.blocks, self.send, self.recv, self.x, self.y = own, part, blocks, send, recv, x, y

    def first(self):
        for dx, dy in FAR_FIRST:
            recv = self.recv.at[(SIDE - dx) % SIDE] if len(self.recv.shape) else self.recv
            remote(self.own, self.part, self.send, recv, "row",
                   lax.rem(self.x + dx, SIDE) * SIDE + lax.rem(self.y + dy, SIDE)).start()

    def wait(self):
        taken(self.blocks(SIDE * SIDE - 1), self.recv)

    def wait_x(self, dx):
        @pl.when(dx == 0)
        def _():
            taken(self.blocks(SIDE - 1), self.recv.at[0])

        @pl.when(dx != 0)
        def _():
            taken(self.blocks(SIDE), self.recv.at[dx])

    def finish(self):
        taken(self.blocks(SIDE * SIDE - 1), self.send)


class Mixed:
    def __init__(self, own, part, blocks, sems, x, y):
        self.own, self.part, self.blocks, self.sems, self.x, self.y = own, part, blocks, sems, x, y

    def at(self, dx, dy):
        return lax.rem(self.x + dx, SIDE) * SIDE + lax.rem(self.y + dy, SIDE)

    def send(self, block, place, ox, oy, dx, dy):
        sem = SIDE if (ox, oy) == (0, 2) else SIDE + 1 if (ox, oy) == (2, 0) else ox
        remote(block, place, self.sems.at[SIDE + 2], self.sems.at[sem], "row", self.at(dx, dy)).start()

    def first(self):
        for dx, dy in ((2, 0), (0, 2), (2, 2), (1, 1), (3, 3), (1, 3), (3, 1), (0, 1), (1, 0), (0, 3), (3, 0)):
            self.send(self.own, self.part(self.at(0, 0)), -dx % SIDE, -dy % SIDE, dx, dy)

    def forward(self):
        for k, (ox, oy) in enumerate(((0, 2), (2, 0))):
            taken(self.blocks(1), self.sems.at[SIDE + k])
            block = self.part(self.at(ox, oy))
            for d in (1, 3):
                dx, dy = (d, 0) if ox == 0 else (0, d)
                self.send(block, block, (ox - dx) % SIDE, (oy - dy) % SIDE, dx, dy)

    def wait_x(self, dx):
        @pl.when(dx == 0)
        def _():
            taken(self.blocks(2), self.sems.at[0])

        @pl.when(dx == 2)
        def _():
            taken(self.blocks(3), self.sems.at[2])

        @pl.when((dx != 0) & (dx != 2))
        def _():
            taken(self.blocks(4), self.sems.at[dx])

    def finish(self):
        taken(self.blocks(SIDE * SIDE - 1), self.sems.at[SIDE + 2])


def kernel(lens_h, owners_h, act_h, grad_h, pin_h, pout_h, curv_h, store_h, out_ref,
           lens, owners, rowsv, proj, curv, store, res, limits, acc, spread, ready, feats, pres, slots_hot, total, score, parts,
           in_sem, own_sem, sems1, sems2, last1, sems3):
    mods, rows = lax.axis_size("mod"), lax.axis_size("row")
    mod_id, row_id = lax.axis_index("mod"), lax.axis_index("row")
    x, y = row_id // SIDE, lax.rem(row_id, SIDE)
    tokens, width = rowsv.shape[1:]
    rank = proj.shape[1]
    entries = rank * rank
    queries = lens_h.shape[1]
    share = curv.shape[0]
    tile = tokens // TILES
    LAST = TILES - 1

    tile_sem, proj_sem, late_sem, small_sem = in_sem
    small = [pltpu.make_async_copy(lens_h, lens, small_sem.at[0]), pltpu.make_async_copy(owners_h, owners, small_sem.at[1])]
    projs = [pltpu.make_async_copy(h.at[0], proj.at[m], proj_sem.at[m]) for m, h in enumerate((pin_h, pout_h))]
    late = [pltpu.make_async_copy(curv_h.at[0], curv, late_sem.at[0]), pltpu.make_async_copy(store_h.at[0], store, late_sem.at[1])]

    def tile_copy(m, t):
        at = pl.ds(pl.multiple_of(t * tile, tile), tile)
        return pltpu.make_async_copy((act_h, grad_h)[m].at[0, at], rowsv.at[m, at], tile_sem.at[m, t])

    small[0].start()
    small[1].start()
    for m in (0, 1):
        projs[m].start()
        tile_copy(m, 0).start()

    def fetch_tile(t, _):
        tile_copy(0, t).start()
        tile_copy(1, t).start()
        return 0
    lax.fori_loop(1, TILES, fetch_tile, 0)

    barrier = pltpu.get_barrier_semaphore()

    def greet(axis, me, n):
        def step(d, _):
            pl.semaphore_signal(barrier, inc=1, device_id={axis: lax.rem(me + d, n)}, device_id_type=pl.DeviceIdType.MESH)
            return 0
        lax.fori_loop(1, n, step, 0)
    greet("row", row_id, rows)
    greet("mod", mod_id, mods)

    small[0].wait()
    small[1].wait()
    i0 = lax.broadcasted_iota(jnp.int32, (queries, queries), 0)
    i1 = lax.broadcasted_iota(jnp.int32, (queries, queries), 1)
    own_r = owners[...]
    len_r = lens[...]
    own_rb = jnp.broadcast_to(own_r, (queries, queries))
    len_rb = jnp.broadcast_to(len_r, (queries, queries))
    own_c = jnp.sum(jnp.where(i0 == i1, own_rb, 0), axis=1, keepdims=True)
    len_c = jnp.sum(jnp.where(i0 == i1, len_rb, 0), axis=1, keepdims=True)
    same = own_c == own_rb
    before_c = same & (i1 < i0)
    before_r = same & (i0 < i1)
    rank_c = jnp.sum(jnp.where(before_c, 1, 0), axis=1, keepdims=True)
    rank_r = jnp.sum(jnp.where(before_r, 1, 0), axis=0, keepdims=True)
    off_r = jnp.sum(jnp.where(before_r, jnp.broadcast_to(len_c, (queries, queries)), 0), axis=0, keepdims=True)
    s0 = lax.broadcasted_iota(jnp.int32, (CAP, queries), 0)
    chosen = (jnp.broadcast_to(rank_r, (CAP, queries)) == s0) & (jnp.broadcast_to(own_r, (CAP, queries)) == row_id)
    begin = jnp.sum(jnp.where(chosen, jnp.broadcast_to(off_r, (CAP, queries)), 0), axis=1, keepdims=True)
    count = jnp.sum(jnp.where(chosen, jnp.broadcast_to(len_r, (CAP, queries)), 0), axis=1, keepdims=True)
    limits[0] = jnp.broadcast_to(begin, limits.shape[1:])
    limits[1] = jnp.broadcast_to(begin + count, limits.shape[1:])
    slot_c = (rank_c // PAIR) * (rows * PAIR) + own_c * PAIR + rank_c % PAIR

    def one_hot(left, right):
        return jnp.where(left == right, 1.0, 0.0).astype(bf16)

    def along(n, m, axis):
        return lax.broadcasted_iota(jnp.int32, (n, m), axis)

    slots_hot[...] = one_hot(jnp.broadcast_to(slot_c, slots_hot.shape), along(*slots_hot.shape, 1))

    def row_pair(r):
        return pl.ds(pl.multiple_of(r * PAIR, PAIR), PAIR)

    def ready_like(n):
        return pres.at[pl.ds(0, n), pl.ds(0, queries // 2)]

    def features(t):
        half = entries // 2
        return Gather(lambda h: ready.at[t, pl.ds(0, PAIR), pl.ds(h * half, half)],
                      lambda h, r: feats.at[t, row_pair(r), pl.ds(h * half, half)],
                      lambda n: ready_like(n), sems1.at[t], x, y)

    def straight(t):
        return Direct(ready.at[t, pl.ds(0, PAIR)], feats.at[t, row_pair(row_id)], ready_like, last1.at[t - RELAYED, 1],
                      last1.at[t - RELAYED, 0], x, y)

    pre_rows = Mixed(pres.at[row_id], lambda r: pres.at[r], lambda n: pres.at[pl.ds(0, n)], sems2, x, y)

    def own(t):
        return pltpu.make_async_copy(ready.at[t, pl.ds(0, PAIR)], feats.at[t, row_pair(row_id)], own_sem.at[t])

    acc[...] = jnp.zeros_like(acc)
    projs[0].wait()
    projs[1].wait()

    def token_tile(t, _):
        at = pl.ds(pl.multiple_of(t * tile, tile), tile)

        def side(m, _):
            pltpu.make_async_copy(act_h.at[0, at], rowsv.at[m, at], tile_sem.at[m, t]).wait()
            res[m] = dot_nt(rowsv[m, at, :], proj[m])
            return 0
        lax.fori_loop(0, 2, side, 0)

        @pl.when(t == 1)
        def _():
            late[0].start()
            late[1].start()

        @pl.when(t == 0)
        def _():
            pl.semaphore_wait(barrier, rows - 1 + mods - 1)

        @pl.when(t >= 2)
        def _():
            features(t - 2).forward_far()

        in_hi, in_lo = halves(res[0])
        in_hi = jnp.concatenate([in_hi, in_hi], axis=1)
        in_lo = jnp.concatenate([in_lo, in_lo], axis=1)
        right = jnp.concatenate([jnp.concatenate([in_hi, in_lo], axis=1)] * 2, axis=0)
        fout_t = res[1].T
        pos = lax.broadcasted_iota(jnp.int32, (CAP, tile), 1) + t * tile
        member = jnp.where((pos >= limits[0]) & (pos < limits[1]), 1.0, 0.0)
        member = member.astype(bf16)
        out_hi, out_lo = halves(fout_t)
        left = []
        for s in range(CAP):
            m = jnp.broadcast_to(member[s:s + 1, :], out_hi.shape)
            left.append(jnp.concatenate([out_hi * m, out_lo * m], axis=1))
        g = dot_nn(jnp.concatenate(left, axis=0), right)
        acc[...] = acc[...] + (g[:, :2 * rank] + g[:, 2 * rank:])
        lane = lax.broadcasted_iota(jnp.int32, (rank // 2, 2 * rank), 1)
        for p in range(PAIR):
            base = pl.multiple_of((t * PAIR + p) * rank, rank)
            even = acc[pl.ds(base, rank // 2, stride=2), :]
            odd = acc[pl.ds(base + 1, rank // 2, stride=2), :]
            spread[:, p, :] = jnp.where(lane < rank, even, odd)
        for r in range(rank // 2):
            ready[t, 0:PAIR, r * 128:(r + 1) * 128] = spread[r, 0:PAIR, :].astype(bf16)

        own(t).start()

        @pl.when(t < RELAYED)
        def _():
            features(t).first()

        @pl.when(t >= RELAYED)
        def _():
            straight(t).first()

        @pl.when(t >= 1)
        def _():
            features(t - 1).forward_near()
        return 0
    lax.fori_loop(0, TILES, token_tile, 0)

    late[0].wait()
    late[1].wait()
    features(LAST - 1).forward_far()
    for t in range(TILES):
        (features(t) if t < RELAYED else straight(t)).wait()
        own(t).wait()
    turned = dot_nt(curv[...], jnp.concatenate([feats[t] for t in range(TILES)], axis=0)).astype(bf16)
    pres[row_id] = dot_nt(slots_hot[...], turned).astype(bf16)
    pre_rows.first()
    pre_rows.forward()
    total[...] = jnp.zeros_like(total)

    def source(dx, _):
        pre_rows.wait_x(dx)
        r = lax.rem(x + dx, SIDE) * SIDE
        left = [pres[r + k] for k in range(SIDE)]
        right = store[:, pl.ds(pl.multiple_of(r * share, SIDE * share), SIDE * share)]
        total[...] = total[...] + dot_nt(right, jnp.concatenate(left, axis=1))
        return 0
    lax.fori_loop(0, SIDE, source, 0)

    score[...] = total[...].T.astype(bf16).reshape(score.shape)

    for d in (4, 5, 3, 2, 6, 7, 1):
        peer = lax.rem(mod_id + d, mods)
        remote(score.at[peer], parts.at[mod_id], sems3.at[0], sems3.at[1], "mod", peer).start()
    parts[mod_id] = score[mod_id]
    for t in range(TILES):
        (features(t) if t < RELAYED else straight(t)).finish()
    pre_rows.finish()
    taken(parts.at[pl.ds(0, mods - 1)], sems3.at[1])
    summed = parts[0].astype(f32)
    for m in range(1, mods):
        summed = summed + parts[m].astype(f32)
    out_ref[...] = summed

    taken(score.at[pl.ds(0, mods - 1)], sems3.at[0])


def on_device(activations, out_grads, in_projection, out_projection, inv_curvature, store_grads, lengths, owners):
    _, tokens, width = activations.shape
    rank = in_projection.shape[1]
    queries = lengths.shape[0]
    mods, rows = lax.axis_size("mod"), lax.axis_size("row")
    held, depth = store_grads.shape[1], store_grads.shape[2]
    share = inv_curvature.shape[1]
    hbm = pl.BlockSpec(memory_space=pl.ANY)
    vmem = pl.BlockSpec(memory_space=pltpu.VMEM)
    dma = pltpu.SemaphoreType.DMA
    return pl.pallas_call(
        kernel,
        out_shape=pltpu.VMEM((queries // mods, held), f32),
        in_specs=[hbm] * 8,
        out_specs=vmem,
        scratch_shapes=[
            pltpu.VMEM((1, queries), jnp.int32),
            pltpu.VMEM((1, queries), jnp.int32),
            pltpu.VMEM((2, tokens, width), bf16),
            pltpu.VMEM((2, rank, width), bf16),
            pltpu.VMEM((share, depth), bf16),
            pltpu.VMEM((held, depth), bf16),
            pltpu.VMEM((2, tokens // TILES, rank), f32),
            pltpu.VMEM((2, CAP, tokens // TILES), jnp.int32),
            pltpu.VMEM((CAP * rank, 2 * rank), f32),
            pltpu.VMEM((rank // 2, CAP, 2 * rank), f32),
            pltpu.VMEM((TILES, CAP, rank * rank), bf16),
            pltpu.VMEM((TILES, rows * PAIR, rank * rank), bf16),
            pltpu.VMEM((rows, queries, share), bf16),
            pltpu.VMEM((queries, rows * CAP), bf16),
            pltpu.VMEM((held, queries), f32),
            pltpu.VMEM((mods, queries // mods, held), bf16),
            pltpu.VMEM((mods, queries // mods, held), bf16),
            (dma((2, TILES)), dma((2,)), dma((2,)), dma((2,))),
            dma((TILES,)),
            dma((max(RELAYED,1), 4)), dma((SIDE + 3,)),
            dma((TILES - RELAYED, 2)),
            dma((2,)),
        ],
        compiler_params=pltpu.CompilerParams(collective_id=0, has_side_effects=True, vmem_limit_bytes=60 * 1024 * 1024),
    )(lengths.reshape(1, queries), owners.reshape(1, queries), activations, out_grads, in_projection,
      out_projection, inv_curvature, store_grads)


def solution(mesh):
    return jax.shard_map(
        on_device,
        mesh=mesh,
        in_specs=(
            P("mod", "row", None),
            P("mod", "row", None),
            P("mod", None, None),
            P("mod", None, None),
            P("mod", "row", None),
            P("mod", "row", None),
            P(),
            P(),
        ),
        out_specs=P("mod", "row"),
        check_vma=False,
    )
```

```python
import jax
import jax.numpy as jnp
from jax import lax
from jax.experimental import pallas as pl
from jax.experimental.pallas import tpu as pltpu
from jax.sharding import PartitionSpec as P

f32, bf16 = jnp.float32, jnp.bfloat16
CAP = 8
LEN_MAX, LEN_MIN = 128, 64
TILES = 4
RELAYED = 3
PAIR = CAP // TILES
SIDE = 4
FAR_FIRST = sorted(((dx, dy) for dx in range(SIDE) for dy in range(SIDE) if dx or dy),
                   key=lambda d: -sum(min(c, SIDE - c) for c in d))


def dot_nt(a, b):
    return lax.dot_general(a, b, (((1,), (1,)), ((), ())), preferred_element_type=f32)


def dot_nn(a, b):
    return lax.dot_general(a, b, (((1,), (0,)), ((), ())), preferred_element_type=f32)


def halves(x):
    hi = x.astype(bf16)
    return hi, (x - hi.astype(f32)).astype(bf16)


def remote(src, dst, send, recv, axis, peer):
    return pltpu.make_async_remote_copy(
        src_ref=src, dst_ref=dst, send_sem=send, recv_sem=recv,
        device_id={axis: peer}, device_id_type=pl.DeviceIdType.MESH,
    )


def taken(ref, sem):
    pltpu.make_async_copy(ref, ref, sem).wait()


class Gather:
    def __init__(self, own, part, blocks, sems, x, y):
        self.own, self.part, self.blocks, self.x, self.y = own, part, blocks, x, y
        self.send, self.near, self.far, self.rest = (sems.at[i] for i in range(4))

    def at(self, h, d1, d2):
        dx, dy = (d2, d1) if h == 0 else (d1, d2)
        return lax.rem(self.x + dx, SIDE) * SIDE + lax.rem(self.y + dy, SIDE)

    def first(self):
        for d, sem in ((1, self.near), (3, self.near), (2, self.far)):
            for h in (0, 1):
                place = self.part(h, self.at(h, 0, 0))
                remote(self.own(h), place, self.send, sem, "row", self.at(h, d, 0)).start()
        for h in (0, 1):
            self.onward(h, 0, self.own(h))

    def onward(self, h, e, block):
        place = self.part(h, self.at(h, e, 0))

        def to(d, _):
            remote(block, place, self.send, self.rest, "row", self.at(h, 0, d)).start()
            return 0
        lax.fori_loop(1, SIDE, to, 0)

    def forward_near(self):
        taken(self.blocks(2), self.near)
        for h in (0, 1):
            for e in (1, 3):
                self.onward(h, e, self.part(h, self.at(h, e, 0)))

    def forward_far(self):
        taken(self.blocks(1), self.far)
        for h in (0, 1):
            self.onward(h, 2, self.part(h, self.at(h, 2, 0)))

    def wait(self):
        taken(self.blocks(12), self.rest)

    def finish(self):
        taken(self.blocks(15), self.send)


class Direct:
    def __init__(self, own, part, blocks, send, recv, x, y):
        self.own, self.part, self.blocks, self.send, self.recv, self.x, self.y = own, part, blocks, send, recv, x, y

    def first(self):
        for dx, dy in FAR_FIRST:
            recv = self.recv.at[(SIDE - dx) % SIDE] if len(self.recv.shape) else self.recv
            remote(self.own, self.part, self.send, recv, "row",
                   lax.rem(self.x + dx, SIDE) * SIDE + lax.rem(self.y + dy, SIDE)).start()

    def wait(self):
        taken(self.blocks(SIDE * SIDE - 1), self.recv)

    def wait_x(self, dx):
        @pl.when(dx == 0)
        def _():
            taken(self.blocks(SIDE - 1), self.recv.at[0])

        @pl.when(dx != 0)
        def _():
            taken(self.blocks(SIDE), self.recv.at[dx])

    def finish(self):
        taken(self.blocks(SIDE * SIDE - 1), self.send)


class Mixed:
    def __init__(self, own, part, blocks, sems, x, y):
        self.own, self.part, self.blocks, self.sems, self.x, self.y = own, part, blocks, sems, x, y

    def at(self, dx, dy):
        return lax.rem(self.x + dx, SIDE) * SIDE + lax.rem(self.y + dy, SIDE)

    def send(self, block, place, ox, oy, dx, dy):
        sem = SIDE if (ox, oy) == (0, 2) else SIDE + 1 if (ox, oy) == (2, 0) else ox
        remote(block, place, self.sems.at[SIDE + 2], self.sems.at[sem], "row", self.at(dx, dy)).start()

    def first(self):
        for dx, dy in ((2, 0), (0, 2), (2, 2), (1, 1), (3, 3), (1, 3), (3, 1), (0, 1), (1, 0), (0, 3), (3, 0)):
            self.send(self.own, self.part(self.at(0, 0)), -dx % SIDE, -dy % SIDE, dx, dy)

    def forward(self):
        for k, (ox, oy) in enumerate(((0, 2), (2, 0))):
            taken(self.blocks(1), self.sems.at[SIDE + k])
            block = self.part(self.at(ox, oy))
            for d in (1, 3):
                dx, dy = (d, 0) if ox == 0 else (0, d)
                self.send(block, block, (ox - dx) % SIDE, (oy - dy) % SIDE, dx, dy)

    def wait_x(self, dx):
        @pl.when(dx == 0)
        def _():
            taken(self.blocks(2), self.sems.at[0])

        @pl.when(dx == 2)
        def _():
            taken(self.blocks(3), self.sems.at[2])

        @pl.when((dx != 0) & (dx != 2))
        def _():
            taken(self.blocks(4), self.sems.at[dx])

    def finish(self):
        taken(self.blocks(SIDE * SIDE - 1), self.sems.at[SIDE + 2])


def kernel(lens_h, owners_h, act_h, grad_h, pin_h, pout_h, curv_h, store_h, out_ref,
           lens, owners, rowsv, proj, curv, store, res, limits, acc, spread, ready, feats, pres, slots_hot, total, score, parts,
           in_sem, own_sem, sems1, sems2, last1, sems3):
    mods, rows = lax.axis_size("mod"), lax.axis_size("row")
    mod_id, row_id = lax.axis_index("mod"), lax.axis_index("row")
    x, y = row_id // SIDE, lax.rem(row_id, SIDE)
    tokens, width = rowsv.shape[1:]
    rank = proj.shape[1]
    entries = rank * rank
    queries = lens_h.shape[1]
    share = curv.shape[0]
    tile = tokens // TILES
    LAST = TILES - 1

    tile_sem, proj_sem, late_sem, small_sem = in_sem
    small = [pltpu.make_async_copy(lens_h, lens, small_sem.at[0]), pltpu.make_async_copy(owners_h, owners, small_sem.at[1])]
    projs = [pltpu.make_async_copy(h.at[0], proj.at[m], proj_sem.at[m]) for m, h in enumerate((pin_h, pout_h))]
    late = [pltpu.make_async_copy(curv_h.at[0], curv, late_sem.at[0]), pltpu.make_async_copy(store_h.at[0], store, late_sem.at[1])]

    def tile_copy(m, t):
        at = pl.ds(pl.multiple_of(t * tile, tile), tile)
        return pltpu.make_async_copy((act_h, grad_h)[m].at[0, at], rowsv.at[m, at], tile_sem.at[m, t])

    small[0].start()
    small[1].start()
    for m in (0, 1):
        projs[m].start()
        tile_copy(m, 0).start()

    def fetch_tile(t, _):
        tile_copy(0, t).start()
        tile_copy(1, t).start()
        return 0
    lax.fori_loop(1, TILES, fetch_tile, 0)

    barrier = pltpu.get_barrier_semaphore()

    def greet(axis, me, n):
        def step(d, _):
            pl.semaphore_signal(barrier, inc=1, device_id={axis: lax.rem(me + d, n)}, device_id_type=pl.DeviceIdType.MESH)
            return 0
        lax.fori_loop(1, n, step, 0)
    greet("row", row_id, rows)
    greet("mod", mod_id, mods)

    small[0].wait()
    small[1].wait()
    i0 = lax.broadcasted_iota(jnp.int32, (queries, queries), 0)
    i1 = lax.broadcasted_iota(jnp.int32, (queries, queries), 1)
    own_r = owners[...]
    len_r = lens[...]
    own_rb = jnp.broadcast_to(own_r, (queries, queries))
    len_rb = jnp.broadcast_to(len_r, (queries, queries))
    own_c = jnp.sum(jnp.where(i0 == i1, own_rb, 0), axis=1, keepdims=True)
    len_c = jnp.sum(jnp.where(i0 == i1, len_rb, 0), axis=1, keepdims=True)
    same = own_c == own_rb
    before_c = same & (i1 < i0)
    before_r = same & (i0 < i1)
    rank_c = jnp.sum(jnp.where(before_c, 1, 0), axis=1, keepdims=True)
    rank_r = jnp.sum(jnp.where(before_r, 1, 0), axis=0, keepdims=True)
    off_r = jnp.sum(jnp.where(before_r, jnp.broadcast_to(len_c, (queries, queries)), 0), axis=0, keepdims=True)
    s0 = lax.broadcasted_iota(jnp.int32, (CAP, queries), 0)
    chosen = (jnp.broadcast_to(rank_r, (CAP, queries)) == s0) & (jnp.broadcast_to(own_r, (CAP, queries)) == row_id)
    begin = jnp.sum(jnp.where(chosen, jnp.broadcast_to(off_r, (CAP, queries)), 0), axis=1, keepdims=True)
    count = jnp.sum(jnp.where(chosen, jnp.broadcast_to(len_r, (CAP, queries)), 0), axis=1, keepdims=True)
    limits[0] = jnp.broadcast_to(begin, limits.shape[1:])
    limits[1] = jnp.broadcast_to(begin + count, limits.shape[1:])
    slot_c = (rank_c // PAIR) * (rows * PAIR) + own_c * PAIR + rank_c % PAIR

    def one_hot(left, right):
        return jnp.where(left == right, 1.0, 0.0).astype(bf16)

    def along(n, m, axis):
        return lax.broadcasted_iota(jnp.int32, (n, m), axis)

    slots_hot[...] = one_hot(jnp.broadcast_to(slot_c, slots_hot.shape), along(*slots_hot.shape, 1))

    def row_pair(r):
        return pl.ds(pl.multiple_of(r * PAIR, PAIR), PAIR)

    def ready_like(n):
        return pres.at[pl.ds(0, n), pl.ds(0, queries // 2)]

    def features(t):
        half = entries // 2
        return Gather(lambda h: ready.at[t, pl.ds(0, PAIR), pl.ds(h * half, half)],
                      lambda h, r: feats.at[t, row_pair(r), pl.ds(h * half, half)],
                      lambda n: ready_like(n), sems1.at[t], x, y)

    def straight(t):
        return Direct(ready.at[t, pl.ds(0, PAIR)], feats.at[t, row_pair(row_id)], ready_like, last1.at[t - RELAYED, 1],
                      last1.at[t - RELAYED, 0], x, y)

    pre_rows = Mixed(pres.at[row_id], lambda r: pres.at[r], lambda n: pres.at[pl.ds(0, n)], sems2, x, y)

    def own(t):
        return pltpu.make_async_copy(ready.at[t, pl.ds(0, PAIR)], feats.at[t, row_pair(row_id)], own_sem.at[t])

    acc[...] = jnp.zeros_like(acc)
    projs[0].wait()
    projs[1].wait()

    def token_tile(t, _):
        at = pl.ds(pl.multiple_of(t * tile, tile), tile)

        def side(m, _):
            pltpu.make_async_copy(act_h.at[0, at], rowsv.at[m, at], tile_sem.at[m, t]).wait()
            res[m] = dot_nt(rowsv[m, at, :], proj[m])
            return 0
        lax.fori_loop(0, 2, side, 0)

        @pl.when(t == 1)
        def _():
            late[0].start()
            late[1].start()

        @pl.when(t == 0)
        def _():
            pl.semaphore_wait(barrier, rows - 1 + mods - 1)

        @pl.when(t >= 2)
        def _():
            features(t - 2).forward_far()

        in_hi, in_lo = halves(res[0])
        in_hi = jnp.concatenate([in_hi, in_hi], axis=1)
        in_lo = jnp.concatenate([in_lo, in_lo], axis=1)
        right = jnp.concatenate([jnp.concatenate([in_hi, in_lo], axis=1)] * 2, axis=0)
        fout_t = res[1].T
        pos = lax.broadcasted_iota(jnp.int32, (CAP, tile), 1) + t * tile
        member = jnp.where((pos >= limits[0]) & (pos < limits[1]), 1.0, 0.0)
        member = member.astype(bf16)
        out_hi, out_lo = halves(fout_t)
        left = []
        for s in range(CAP):
            m = jnp.broadcast_to(member[s:s + 1, :], out_hi.shape)
            left.append(jnp.concatenate([out_hi * m, out_lo * m], axis=1))
        g = dot_nn(jnp.concatenate(left, axis=0), right)
        acc[...] = acc[...] + (g[:, :2 * rank] + g[:, 2 * rank:])
        lane = lax.broadcasted_iota(jnp.int32, (rank // 2, 2 * rank), 1)
        for p in range(PAIR):
            base = pl.multiple_of((t * PAIR + p) * rank, rank)
            even = acc[pl.ds(base, rank // 2, stride=2), :]
            odd = acc[pl.ds(base + 1, rank // 2, stride=2), :]
            spread[:, p, :] = jnp.where(lane < rank, even, odd)
        for r in range(rank // 2):
            ready[t, 0:PAIR, r * 128:(r + 1) * 128] = spread[r, 0:PAIR, :].astype(bf16)

        own(t).start()

        @pl.when(t < RELAYED)
        def _():
            features(t).first()

        @pl.when(t >= RELAYED)
        def _():
            straight(t).first()

        @pl.when(t >= 1)
        def _():
            features(t - 1).forward_near()
        return 0
    lax.fori_loop(0, TILES, token_tile, 0)

    features(LAST - 1).forward_far()
    for t in range(TILES):
        (features(t) if t < RELAYED else straight(t)).wait()
        own(t).wait()
    late[0].wait()
    turned = dot_nt(curv[...], jnp.concatenate([feats[t] for t in range(TILES)], axis=0)).astype(bf16)
    pres[row_id] = dot_nt(slots_hot[...], turned).astype(bf16)
    pre_rows.first()
    pre_rows.forward()
    late[1].wait()
    total[...] = jnp.zeros_like(total)

    def source(dx, _):
        pre_rows.wait_x(dx)
        r = lax.rem(x + dx, SIDE) * SIDE
        left = [pres[r + k] for k in range(SIDE)]
        right = store[:, pl.ds(pl.multiple_of(r * share, SIDE * share), SIDE * share)]
        total[...] = total[...] + dot_nt(right, jnp.concatenate(left, axis=1))
        return 0
    lax.fori_loop(0, SIDE, source, 0)

    score[...] = total[...].T.astype(bf16).reshape(score.shape)

    for d in (4, 5, 3, 2, 6, 7, 1):
        peer = lax.rem(mod_id + d, mods)
        remote(score.at[peer], parts.at[mod_id], sems3.at[0], sems3.at[1], "mod", peer).start()
    parts[mod_id] = score[mod_id]
    for t in range(TILES):
        (features(t) if t < RELAYED else straight(t)).finish()
    pre_rows.finish()
    taken(parts.at[pl.ds(0, mods - 1)], sems3.at[1])
    summed = parts[0].astype(f32)
    for m in range(1, mods):
        summed = summed + parts[m].astype(f32)
    out_ref[...] = summed

    taken(score.at[pl.ds(0, mods - 1)], sems3.at[0])


def on_device(activations, out_grads, in_projection, out_projection, inv_curvature, store_grads, lengths, owners):
    _, tokens, width = activations.shape
    rank = in_projection.shape[1]
    queries = lengths.shape[0]
    mods, rows = lax.axis_size("mod"), lax.axis_size("row")
    held, depth = store_grads.shape[1], store_grads.shape[2]
    share = inv_curvature.shape[1]
    hbm = pl.BlockSpec(memory_space=pl.ANY)
    vmem = pl.BlockSpec(memory_space=pltpu.VMEM)
    dma = pltpu.SemaphoreType.DMA
    return pl.pallas_call(
        kernel,
        out_shape=pltpu.VMEM((queries // mods, held), f32),
        in_specs=[hbm] * 8,
        out_specs=vmem,
        scratch_shapes=[
            pltpu.VMEM((1, queries), jnp.int32),
            pltpu.VMEM((1, queries), jnp.int32),
            pltpu.VMEM((2, tokens, width), bf16),
            pltpu.VMEM((2, rank, width), bf16),
            pltpu.VMEM((share, depth), bf16),
            pltpu.VMEM((held, depth), bf16),
            pltpu.VMEM((2, tokens // TILES, rank), f32),
            pltpu.VMEM((2, CAP, tokens // TILES), jnp.int32),
            pltpu.VMEM((CAP * rank, 2 * rank), f32),
            pltpu.VMEM((rank // 2, CAP, 2 * rank), f32),
            pltpu.VMEM((TILES, CAP, rank * rank), bf16),
            pltpu.VMEM((TILES, rows * PAIR, rank * rank), bf16),
            pltpu.VMEM((rows, queries, share), bf16),
            pltpu.VMEM((queries, rows * CAP), bf16),
            pltpu.VMEM((held, queries), f32),
            pltpu.VMEM((mods, queries // mods, held), bf16),
            pltpu.VMEM((mods, queries // mods, held), bf16),
            (dma((2, TILES)), dma((2,)), dma((2,)), dma((2,))),
            dma((TILES,)),
            dma((max(RELAYED,1), 4)), dma((SIDE + 3,)),
            dma((TILES - RELAYED, 2)),
            dma((2,)),
        ],
        compiler_params=pltpu.CompilerParams(collective_id=0, has_side_effects=True, vmem_limit_bytes=60 * 1024 * 1024),
    )(lengths.reshape(1, queries), owners.reshape(1, queries), activations, out_grads, in_projection,
      out_projection, inv_curvature, store_grads)


def solution(mesh):
    return jax.shard_map(
        on_device,
        mesh=mesh,
        in_specs=(
            P("mod", "row", None),
            P("mod", "row", None),
            P("mod", None, None),
            P("mod", None, None),
            P("mod", "row", None),
            P("mod", "row", None),
            P(),
            P(),
        ),
        out_specs=P("mod", "row"),
        check_vma=False,
    )
```

```python
import jax
import jax.numpy as jnp
from jax import lax
from jax.experimental import pallas as pl
from jax.experimental.pallas import tpu as pltpu
from jax.sharding import PartitionSpec as P

f32, bf16 = jnp.float32, jnp.bfloat16
CAP = 8
LEN_MAX, LEN_MIN = 128, 64
TILES = 4
RELAYED = 3
PAIR = CAP // TILES
SIDE = 4
FAR_FIRST = sorted(((dx, dy) for dx in range(SIDE) for dy in range(SIDE) if dx or dy),
                   key=lambda d: -sum(min(c, SIDE - c) for c in d))


def dot_nt(a, b):
    return lax.dot_general(a, b, (((1,), (1,)), ((), ())), preferred_element_type=f32)


def dot_nn(a, b):
    return lax.dot_general(a, b, (((1,), (0,)), ((), ())), preferred_element_type=f32)


def halves(x):
    hi = x.astype(bf16)
    return hi, (x - hi.astype(f32)).astype(bf16)


def remote(src, dst, send, recv, axis, peer):
    return pltpu.make_async_remote_copy(
        src_ref=src, dst_ref=dst, send_sem=send, recv_sem=recv,
        device_id={axis: peer}, device_id_type=pl.DeviceIdType.MESH,
    )


def taken(ref, sem):
    pltpu.make_async_copy(ref, ref, sem).wait()


class Gather:
    def __init__(self, own, part, blocks, sems, x, y):
        self.own, self.part, self.blocks, self.x, self.y = own, part, blocks, x, y
        self.send, self.near, self.far, self.rest = (sems.at[i] for i in range(4))

    def at(self, h, d1, d2):
        dx, dy = (d2, d1) if h == 0 else (d1, d2)
        return lax.rem(self.x + dx, SIDE) * SIDE + lax.rem(self.y + dy, SIDE)

    def first(self):
        for d, sem in ((1, self.near), (3, self.near), (2, self.far)):
            for h in (0, 1):
                place = self.part(h, self.at(h, 0, 0))
                remote(self.own(h), place, self.send, sem, "row", self.at(h, d, 0)).start()
        for h in (0, 1):
            self.onward(h, 0, self.own(h))

    def onward(self, h, e, block):
        place = self.part(h, self.at(h, e, 0))

        def to(d, _):
            remote(block, place, self.send, self.rest, "row", self.at(h, 0, d)).start()
            return 0
        lax.fori_loop(1, SIDE, to, 0)

    def forward_near(self):
        taken(self.blocks(2), self.near)
        for h in (0, 1):
            for e in (1, 3):
                self.onward(h, e, self.part(h, self.at(h, e, 0)))

    def forward_far(self):
        taken(self.blocks(1), self.far)
        for h in (0, 1):
            self.onward(h, 2, self.part(h, self.at(h, 2, 0)))

    def wait(self):
        taken(self.blocks(12), self.rest)

    def finish(self):
        taken(self.blocks(15), self.send)


class Direct:
    def __init__(self, own, part, blocks, send, recv, x, y):
        self.own, self.part, self.blocks, self.send, self.recv, self.x, self.y = own, part, blocks, send, recv, x, y

    def first(self):
        for dx, dy in FAR_FIRST:
            recv = self.recv.at[(SIDE - dx) % SIDE] if len(self.recv.shape) else self.recv
            remote(self.own, self.part, self.send, recv, "row",
                   lax.rem(self.x + dx, SIDE) * SIDE + lax.rem(self.y + dy, SIDE)).start()

    def wait(self):
        taken(self.blocks(SIDE * SIDE - 1), self.recv)

    def wait_x(self, dx):
        @pl.when(dx == 0)
        def _():
            taken(self.blocks(SIDE - 1), self.recv.at[0])

        @pl.when(dx != 0)
        def _():
            taken(self.blocks(SIDE), self.recv.at[dx])

    def finish(self):
        taken(self.blocks(SIDE * SIDE - 1), self.send)


class Mixed:
    def __init__(self, own, part, blocks, sems, x, y):
        self.own, self.part, self.blocks, self.sems, self.x, self.y = own, part, blocks, sems, x, y

    def at(self, dx, dy):
        return lax.rem(self.x + dx, SIDE) * SIDE + lax.rem(self.y + dy, SIDE)

    def send(self, block, place, ox, oy, dx, dy):
        sem = SIDE if (ox, oy) == (0, 2) else SIDE + 1 if (ox, oy) == (2, 0) else ox
        remote(block, place, self.sems.at[SIDE + 2], self.sems.at[sem], "row", self.at(dx, dy)).start()

    def first(self):
        for dx, dy in ((2, 0), (0, 2), (2, 2), (1, 1), (3, 3), (1, 3), (3, 1), (0, 1), (1, 0), (0, 3), (3, 0)):
            self.send(self.own, self.part(self.at(0, 0)), -dx % SIDE, -dy % SIDE, dx, dy)

    def forward(self):
        for k, (ox, oy) in enumerate(((0, 2), (2, 0))):
            taken(self.blocks(1), self.sems.at[SIDE + k])
            block = self.part(self.at(ox, oy))
            for d in (1, 3):
                dx, dy = (d, 0) if ox == 0 else (0, d)
                self.send(block, block, (ox - dx) % SIDE, (oy - dy) % SIDE, dx, dy)

    def wait_x(self, dx):
        @pl.when(dx == 0)
        def _():
            taken(self.blocks(2), self.sems.at[0])

        @pl.when(dx == 2)
        def _():
            taken(self.blocks(3), self.sems.at[2])

        @pl.when((dx != 0) & (dx != 2))
        def _():
            taken(self.blocks(4), self.sems.at[dx])

    def finish(self):
        taken(self.blocks(SIDE * SIDE - 1), self.sems.at[SIDE + 2])


def kernel(lens_h, owners_h, act_h, grad_h, pin_h, pout_h, curv_h, store_h, out_ref,
           lens, owners, rowsv, proj, curv, store, res, limits, acc, spread, ready, feats, pres, slots_hot, total, score, parts,
           in_sem, own_sem, sems1, sems2, last1, sems3):
    mods, rows = lax.axis_size("mod"), lax.axis_size("row")
    mod_id, row_id = lax.axis_index("mod"), lax.axis_index("row")
    x, y = row_id // SIDE, lax.rem(row_id, SIDE)
    tokens, width = rowsv.shape[1:]
    rank = proj.shape[1]
    entries = rank * rank
    queries = lens_h.shape[1]
    share = curv.shape[0]
    tile = tokens // TILES
    LAST = TILES - 1

    tile_sem, proj_sem, late_sem, small_sem = in_sem
    small = [pltpu.make_async_copy(lens_h, lens, small_sem.at[0]), pltpu.make_async_copy(owners_h, owners, small_sem.at[1])]
    projs = [pltpu.make_async_copy(h.at[0], proj.at[m], proj_sem.at[m]) for m, h in enumerate((pin_h, pout_h))]
    late = [pltpu.make_async_copy(curv_h.at[0], curv, late_sem.at[0]), pltpu.make_async_copy(store_h.at[0], store, late_sem.at[1])]

    def tile_copy(m, t):
        at = pl.ds(pl.multiple_of(t * tile, tile), tile)
        return pltpu.make_async_copy((act_h, grad_h)[m].at[0, at], rowsv.at[m, at], tile_sem.at[m, t])

    small[0].start()
    small[1].start()
    for m in (0, 1):
        projs[m].start()
        tile_copy(m, 0).start()

    def fetch_tile(t, _):
        tile_copy(0, t).start()
        tile_copy(1, t).start()
        return 0
    lax.fori_loop(1, TILES, fetch_tile, 0)

    barrier = pltpu.get_barrier_semaphore()

    def greet(axis, me, n):
        def step(d, _):
            pl.semaphore_signal(barrier, inc=1, device_id={axis: lax.rem(me + d, n)}, device_id_type=pl.DeviceIdType.MESH)
            return 0
        lax.fori_loop(1, n, step, 0)
    greet("row", row_id, rows)
    greet("mod", mod_id, mods)

    small[0].wait()
    small[1].wait()
    i0 = lax.broadcasted_iota(jnp.int32, (queries, queries), 0)
    i1 = lax.broadcasted_iota(jnp.int32, (queries, queries), 1)
    own_r = owners[...]
    len_r = lens[...]
    own_rb = jnp.broadcast_to(own_r, (queries, queries))
    len_rb = jnp.broadcast_to(len_r, (queries, queries))
    own_c = jnp.sum(jnp.where(i0 == i1, own_rb, 0), axis=1, keepdims=True)
    len_c = jnp.sum(jnp.where(i0 == i1, len_rb, 0), axis=1, keepdims=True)
    same = own_c == own_rb
    before_c = same & (i1 < i0)
    before_r = same & (i0 < i1)
    rank_c = jnp.sum(jnp.where(before_c, 1, 0), axis=1, keepdims=True)
    rank_r = jnp.sum(jnp.where(before_r, 1, 0), axis=0, keepdims=True)
    off_r = jnp.sum(jnp.where(before_r, jnp.broadcast_to(len_c, (queries, queries)), 0), axis=0, keepdims=True)
    s0 = lax.broadcasted_iota(jnp.int32, (CAP, queries), 0)
    chosen = (jnp.broadcast_to(rank_r, (CAP, queries)) == s0) & (jnp.broadcast_to(own_r, (CAP, queries)) == row_id)
    begin = jnp.sum(jnp.where(chosen, jnp.broadcast_to(off_r, (CAP, queries)), 0), axis=1, keepdims=True)
    count = jnp.sum(jnp.where(chosen, jnp.broadcast_to(len_r, (CAP, queries)), 0), axis=1, keepdims=True)
    limits[0] = jnp.broadcast_to(begin, limits.shape[1:])
    limits[1] = jnp.broadcast_to(begin + count, limits.shape[1:])
    slot_c = (rank_c // PAIR) * (rows * PAIR) + own_c * PAIR + rank_c % PAIR

    def one_hot(left, right):
        return jnp.where(left == right, 1.0, 0.0).astype(bf16)

    def along(n, m, axis):
        return lax.broadcasted_iota(jnp.int32, (n, m), axis)

    slots_hot[...] = one_hot(jnp.broadcast_to(slot_c, slots_hot.shape), along(*slots_hot.shape, 1))

    def row_pair(r):
        return pl.ds(pl.multiple_of(r * PAIR, PAIR), PAIR)

    def ready_like(n):
        return pres.at[pl.ds(0, n), pl.ds(0, queries // 2)]

    def features(t):
        half = entries // 2
        return Gather(lambda h: ready.at[t, pl.ds(0, PAIR), pl.ds(h * half, half)],
                      lambda h, r: feats.at[t, row_pair(r), pl.ds(h * half, half)],
                      lambda n: ready_like(n), sems1.at[t], x, y)

    def straight(t):
        return Direct(ready.at[t, pl.ds(0, PAIR)], feats.at[t, row_pair(row_id)], ready_like, last1.at[t - RELAYED, 1],
                      last1.at[t - RELAYED, 0], x, y)

    pre_rows = Mixed(pres.at[row_id], lambda r: pres.at[r], lambda n: pres.at[pl.ds(0, n)], sems2, x, y)

    def own(t):
        return pltpu.make_async_copy(ready.at[t, pl.ds(0, PAIR)], feats.at[t, row_pair(row_id)], own_sem.at[t])

    acc[...] = jnp.zeros_like(acc)
    projs[0].wait()
    projs[1].wait()

    def token_tile(t, _):
        at = pl.ds(pl.multiple_of(t * tile, tile), tile)

        def side(m, _):
            pltpu.make_async_copy(act_h.at[0, at], rowsv.at[m, at], tile_sem.at[m, t]).wait()
            res[m] = dot_nt(rowsv[m, at, :], proj[m])
            return 0
        lax.fori_loop(0, 2, side, 0)

        @pl.when(t == 1)
        def _():
            late[0].start()
            late[1].start()

        @pl.when(t == 0)
        def _():
            pl.semaphore_wait(barrier, rows - 1 + mods - 1)

        @pl.when(t >= 2)
        def _():
            features(t - 2).forward_near()
            features(t - 2).forward_far()

        in_hi, in_lo = halves(res[0])
        in_hi = jnp.concatenate([in_hi, in_hi], axis=1)
        in_lo = jnp.concatenate([in_lo, in_lo], axis=1)
        right = jnp.concatenate([jnp.concatenate([in_hi, in_lo], axis=1)] * 2, axis=0)
        fout_t = res[1].T
        pos = lax.broadcasted_iota(jnp.int32, (CAP, tile), 1) + t * tile
        member = jnp.where((pos >= limits[0]) & (pos < limits[1]), 1.0, 0.0)
        member = member.astype(bf16)
        out_hi, out_lo = halves(fout_t)
        left = []
        for s in range(CAP):
            m = jnp.broadcast_to(member[s:s + 1, :], out_hi.shape)
            left.append(jnp.concatenate([out_hi * m, out_lo * m], axis=1))
        g = dot_nn(jnp.concatenate(left, axis=0), right)
        acc[...] = acc[...] + (g[:, :2 * rank] + g[:, 2 * rank:])
        lane = lax.broadcasted_iota(jnp.int32, (rank // 2, 2 * rank), 1)
        for p in range(PAIR):
            base = pl.multiple_of((t * PAIR + p) * rank, rank)
            even = acc[pl.ds(base, rank // 2, stride=2), :]
            odd = acc[pl.ds(base + 1, rank // 2, stride=2), :]
            spread[:, p, :] = jnp.where(lane < rank, even, odd)
        for r in range(rank // 2):
            ready[t, 0:PAIR, r * 128:(r + 1) * 128] = spread[r, 0:PAIR, :].astype(bf16)

        own(t).start()

        @pl.when(t < RELAYED)
        def _():
            features(t).first()

        @pl.when(t >= RELAYED)
        def _():
            straight(t).first()

        return 0
    lax.fori_loop(0, TILES, token_tile, 0)

    features(LAST - 1).forward_near()
    features(LAST - 1).forward_far()
    for t in range(TILES):
        (features(t) if t < RELAYED else straight(t)).wait()
        own(t).wait()
    late[0].wait()
    turned = dot_nt(curv[...], jnp.concatenate([feats[t] for t in range(TILES)], axis=0)).astype(bf16)
    pres[row_id] = dot_nt(slots_hot[...], turned).astype(bf16)
    pre_rows.first()
    pre_rows.forward()
    late[1].wait()
    total[...] = jnp.zeros_like(total)

    def source(dx, _):
        pre_rows.wait_x(dx)
        r = lax.rem(x + dx, SIDE) * SIDE
        left = [pres[r + k] for k in range(SIDE)]
        right = store[:, pl.ds(pl.multiple_of(r * share, SIDE * share), SIDE * share)]
        total[...] = total[...] + dot_nt(right, jnp.concatenate(left, axis=1))
        return 0
    lax.fori_loop(0, SIDE, source, 0)

    score[...] = total[...].T.astype(bf16).reshape(score.shape)

    for d in (4, 5, 3, 2, 6, 7, 1):
        peer = lax.rem(mod_id + d, mods)
        remote(score.at[peer], parts.at[mod_id], sems3.at[0], sems3.at[1], "mod", peer).start()
    parts[mod_id] = score[mod_id]
    for t in range(TILES):
        (features(t) if t < RELAYED else straight(t)).finish()
    pre_rows.finish()
    taken(parts.at[pl.ds(0, mods - 1)], sems3.at[1])
    summed = parts[0].astype(f32)
    for m in range(1, mods):
        summed = summed + parts[m].astype(f32)
    out_ref[...] = summed

    taken(score.at[pl.ds(0, mods - 1)], sems3.at[0])


def on_device(activations, out_grads, in_projection, out_projection, inv_curvature, store_grads, lengths, owners):
    _, tokens, width = activations.shape
    rank = in_projection.shape[1]
    queries = lengths.shape[0]
    mods, rows = lax.axis_size("mod"), lax.axis_size("row")
    held, depth = store_grads.shape[1], store_grads.shape[2]
    share = inv_curvature.shape[1]
    hbm = pl.BlockSpec(memory_space=pl.ANY)
    vmem = pl.BlockSpec(memory_space=pltpu.VMEM)
    dma = pltpu.SemaphoreType.DMA
    return pl.pallas_call(
        kernel,
        out_shape=pltpu.VMEM((queries // mods, held), f32),
        in_specs=[hbm] * 8,
        out_specs=vmem,
        scratch_shapes=[
            pltpu.VMEM((1, queries), jnp.int32),
            pltpu.VMEM((1, queries), jnp.int32),
            pltpu.VMEM((2, tokens, width), bf16),
            pltpu.VMEM((2, rank, width), bf16),
            pltpu.VMEM((share, depth), bf16),
            pltpu.VMEM((held, depth), bf16),
            pltpu.VMEM((2, tokens // TILES, rank), f32),
            pltpu.VMEM((2, CAP, tokens // TILES), jnp.int32),
            pltpu.VMEM((CAP * rank, 2 * rank), f32),
            pltpu.VMEM((rank // 2, CAP, 2 * rank), f32),
            pltpu.VMEM((TILES, CAP, rank * rank), bf16),
            pltpu.VMEM((TILES, rows * PAIR, rank * rank), bf16),
            pltpu.VMEM((rows, queries, share), bf16),
            pltpu.VMEM((queries, rows * CAP), bf16),
            pltpu.VMEM((held, queries), f32),
            pltpu.VMEM((mods, queries // mods, held), bf16),
            pltpu.VMEM((mods, queries // mods, held), bf16),
            (dma((2, TILES)), dma((2,)), dma((2,)), dma((2,))),
            dma((TILES,)),
            dma((max(RELAYED,1), 4)), dma((SIDE + 3,)),
            dma((TILES - RELAYED, 2)),
            dma((2,)),
        ],
        compiler_params=pltpu.CompilerParams(collective_id=0, has_side_effects=True, vmem_limit_bytes=60 * 1024 * 1024),
    )(lengths.reshape(1, queries), owners.reshape(1, queries), activations, out_grads, in_projection,
      out_projection, inv_curvature, store_grads)


def solution(mesh):
    return jax.shard_map(
        on_device,
        mesh=mesh,
        in_specs=(
            P("mod", "row", None),
            P("mod", "row", None),
            P("mod", None, None),
            P("mod", None, None),
            P("mod", "row", None),
            P("mod", "row", None),
            P(),
            P(),
        ),
        out_specs=P("mod", "row"),
        check_vma=False,
    )
```
